32 devices in a mesh: groups: 2 (over x), row: 16 (over z, y, core).
Axes of the slice: x: 2, y: 2, z: 4, core: 2. Of those that a mesh axis runs over, the one named last changes fastest.
Arguments:
- forcing: bfloat16 [16, 32, 512, 256], P(None, None, ('groups', 'row')), parts along dimension 2, may hold values from -6 to 6
- rainfall: float32 [512, 256], P(('groups', 'row')), parts along dimension 0, may hold values from 0.05 to 3
- depth_start: float32 [512, 256], P(('groups', 'row')), parts along dimension 0, may hold values from 0.2 to 2
- observed: float32 [512, 256], P(('groups', 'row')), parts along dimension 0, may hold values from -3.8 to 5.8
- land_mask: int32 [256, 256], P('row'), may hold values from 0 to 1, as said below
- tile_land: int32 [16], replicated, may hold values from 0 to 4096, as said below
- land_rank: int32 [256, 256], P('row'), may hold values from -1 to 4095, as said below
- flow_code: int32 [256, 256], P('row'), may hold values from 0 to 7
- terrain_slope: float32 [256, 256], P('row'), may hold values from 0.01 to 0.3
- input_weight: bfloat16 [256, 32], replicated, may hold values from -1 to 1
- hidden_weight: bfloat16 [256, 64], replicated, may hold values from -0.75 to 0.75
- gate_bias: float32 [256], replicated, may hold values from -3 to 3
- head_weight: float32 [2, 64], replicated, may hold values from -2.4 to 2.4
- head_offset: float32 [2], replicated, may hold values from -1 to 1
Outputs:
- depth_final: float32 [512, 256], P(('groups', 'row')), parts along dimension 0
- misfit: float32 [2], P('groups'), parts along dimension 0
- input_grad: float32 [512, 32], P('groups'), parts along dimension 0
- hidden_grad: float32 [512, 64], P('groups'), parts along dimension 0
- bias_grad: float32 [512], P('groups'), parts along dimension 0
- head_grad: float32 [4, 64], P('groups'), parts along dimension 0
- offset_grad: float32 [4], P('groups'), parts along dimension 0
The draws below stay inside these ranges and needn't reach their ends.
There are 2 independent parts, one for each index of `groups`. The reference program is written for one: setup_inputs(seed, part) draws one part's arguments, and reference() takes and returns one part's arrays. A program takes and returns all parts, laid end to end along the dimension named above; an argument that names none is the same for every part. Nothing has to cross between parts.
Inputs may be any that keep to these rules, and one draw needn't show every extreme that they name: `tile_land`: the counts sum to 32768; some band holds 4096 land cells and some band none. `land_mask`: band t has exactly tile_land[t] cells equal to 1. `land_rank`: in band t the land cells (land_mask 1) carry 0 .. tile_land[t] - 1, each once; sea cells carry -1.
All inputs are finite; a program needn't handle non-finite values.
Results may differ from the reference program's by a relative error of at most 0.00089.
Values may be sent and summed in bfloat16 or wider, within the bound.
No kernel may reach another device: no remote copies, remote signals or barrier semaphores. Data moves between devices by JAX's collectives and lax.ppermute only.
A program may use at most 192 MiB of HBM per device.

```python
import math
import jax
import jax.numpy as jnp
from jax import lax

FEAT = 32
HID = 64
SEQ = 16
SUB = 6
LAND_DEV = 2048
ROWS_DEV = 16
COLS = 256
ROWS = 256
N_ROW = 16


def land_layout(key):
    base = jax.random.fold_in(key, 7301)
    key_order, key_share, key_cells = jax.random.split(base, 3)
    band_cells = ROWS_DEV * COLS
    order = jax.random.permutation(key_order, N_ROW)
    shares = jax.random.randint(key_share, (N_ROW // 2,), 0, 3 * LAND_DEV // 4 + 1)
    shares = shares.at[0].set(LAND_DEV)
    counts = jnp.zeros((N_ROW,), jnp.int32)
    counts = counts.at[order[0::2]].set(LAND_DEV + shares).at[order[1::2]].set(LAND_DEV - shares)
    band_keys = jax.random.split(key_cells, N_ROW)
    positions = jnp.arange(band_cells, dtype=jnp.int32)

    def band_order(band_key):
        return jax.random.permutation(band_key, band_cells)

    def invert(shuffle):
        return jnp.zeros((band_cells,), jnp.int32).at[shuffle].set(positions)
    standing = jax.vmap(invert)(jax.vmap(band_order)(band_keys))
    is_land = standing < counts[:, None]
    ranking = jnp.where(is_land, standing, -1)
    return (counts, is_land.astype(jnp.int32).reshape(ROWS, COLS), ranking.reshape(ROWS, COLS))


def draw_tile_land(key, part):
    return land_layout(key)[0]


def draw_land_mask(key, part):
    return land_layout(key)[1]


def draw_land_rank(key, part):
    return land_layout(key)[2]


def draw_observed(key, part):
    rows_frac = jnp.arange(ROWS, dtype=jnp.float32)[:, None] / ROWS
    spread = 0.3 + 0.9 * rows_frac
    noise = jnp.clip(jax.random.normal(key, (ROWS, COLS), jnp.float32), -4.0, 4.0)
    return 1.0 + noise * spread


def set_ends(array, key, least, largest):
    longest = array.shape.index(max(array.shape))
    spots = []
    for shift in (0, 1):
        where = [jax.random.randint(jax.random.fold_in(key, axis), (), 0, length) for axis, length in enumerate(array.shape)]
        where[longest] = (where[longest] + shift) % array.shape[longest]
        spots.append(tuple(where))
    return array.at[spots[0]].set(least).at[spots[1]].set(largest)


def block_scale(rng, extent, cuts, low, high):
    factor_of, own = 1.0, jax.random.fold_in(rng, 6)
    for dim, blocks in cuts:
        steps = jnp.exp(jax.random.uniform(jax.random.fold_in(own, dim), (blocks,), jnp.float32, low / len(cuts), high / len(cuts)))
        factor_of = factor_of * jnp.repeat(steps, extent[dim] // blocks).reshape([-1 if axis == dim else 1 for axis in range(len(extent))])
    return factor_of


def normal_values(stream_key, extent, scale, reach, cuts=(), kind=jnp.bfloat16):
    gain = block_scale(stream_key, extent, cuts, -0.22, 0.18) if cuts else 1.0
    array = jax.random.normal(stream_key, extent, jnp.float32) * scale * gain
    return jnp.minimum(jnp.maximum(array, -reach), reach).astype(kind)


def setup_inputs(seed: int = 0, part: int = 0) -> dict:
    arg_keys = jax.random.split(jax.random.key(seed), 15)
    part_keys = jax.random.split(jax.random.fold_in(arg_keys[14], part), 15)
    return {
        "forcing": normal_values(part_keys[0], (SEQ, FEAT, ROWS, COLS), 1.0, 6.0, ((2, 16),)),
        "rainfall": jnp.clip(jnp.exp(math.log(3.0) - 4.0943445 * jax.random.uniform(part_keys[1], (ROWS, COLS), jnp.float32) ** block_scale(part_keys[1], (ROWS, COLS), ((0, 16),), -0.2, 0.2)), 0.05, 3.0),
        "depth_start": jnp.clip(0.2 + 1.8 * jax.random.uniform(part_keys[2], (ROWS, COLS), jnp.float32) ** block_scale(part_keys[2], (ROWS, COLS), ((0, 16),), -0.2, 0.2), 0.2, 2.0),
        "observed": draw_observed(jax.random.fold_in(jax.random.fold_in(arg_keys[14], part), 71), part),
        "land_mask": draw_land_mask(jax.random.fold_in(arg_keys[14], 71), part),
        "tile_land": draw_tile_land(jax.random.fold_in(arg_keys[14], 71), part),
        "land_rank": draw_land_rank(jax.random.fold_in(arg_keys[14], 71), part),
        "flow_code": set_ends(jax.random.randint(arg_keys[7], (ROWS, COLS), 0, 8), jax.random.fold_in(arg_keys[7], 1), 0, 7).astype(jnp.int32),
        "terrain_slope": jnp.clip(jnp.exp(math.log(0.3) - 3.4011974 * jax.random.uniform(arg_keys[8], (ROWS, COLS), jnp.float32) ** block_scale(arg_keys[8], (ROWS, COLS), ((0, 16),), -0.2, 0.2)), 0.01, 0.3),
        "input_weight": normal_values(arg_keys[9], (4 * HID, FEAT), FEAT ** -0.5, 1.0),
        "hidden_weight": normal_values(arg_keys[10], (4 * HID, HID), HID ** -0.5, 0.75),
        "gate_bias": normal_values(arg_keys[11], (4 * HID,), 0.5, 3.0, (), jnp.float32),
        "head_weight": normal_values(arg_keys[12], (2, HID), 0.4, 2.4, (), jnp.float32),
        "head_offset": jnp.clip(jax.random.uniform(arg_keys[13], (2,), jnp.float32, -1.0, 1.0), -1.0, 1.0),
    }


compass = ((-1, -1), (-1, 0), (-1, 1), (0, -1), (0, 1), (1, -1), (1, 0), (1, 1))

def cell_forward(input_weight, hidden_weight, gate_bias, inputs):
    hidden_size = hidden_weight.shape[1]
    cell_count = inputs.shape[2]

    def advance(carry, inputs_now):
        state_low, memory, state = carry
        summed = jnp.dot(input_weight, inputs_now, preferred_element_type=jnp.float32)
        summed = summed + jnp.dot(hidden_weight, state_low, preferred_element_type=jnp.float32) + gate_bias[:, None]
        gate_in = jax.nn.sigmoid(summed[:hidden_size])
        gate_keep = jax.nn.sigmoid(summed[hidden_size:2 * hidden_size])
        candidate = jnp.tanh(summed[2 * hidden_size:3 * hidden_size])
        gate_out = jax.nn.sigmoid(summed[3 * hidden_size:])
        memory_new = gate_keep * memory + gate_in * candidate
        state_new = gate_out * jnp.tanh(memory_new)
        gate_values = jnp.concatenate([gate_in, gate_keep, candidate, gate_out], axis=0)
        return ((state_new.astype(jnp.bfloat16), memory_new, state_new), (gate_values, memory_new, state_low))
    start_carry = (jnp.zeros((hidden_size, cell_count), jnp.bfloat16), jnp.zeros((hidden_size, cell_count), jnp.float32), jnp.zeros((hidden_size, cell_count), jnp.float32))
    final_carry, stash = lax.scan(advance, start_carry, inputs)
    return (final_carry[2], stash)

def cell_backward(hidden_weight, inputs, stash, grad_hidden):
    gate_values, memories, states_low = stash
    hidden_size = hidden_weight.shape[1]
    feat_count = inputs.shape[1]
    earlier = jnp.concatenate([jnp.zeros_like(memories[:1]), memories[:-1]], axis=0)
    contract_cells = (((1,), (1,)), ((), ()))

    def retreat(carry, item):
        grad_state, grad_memory, sum_input, sum_hidden, sum_bias = carry
        inputs_now, gate_now, memory_before, memory_now, state_before = item
        gate_in = gate_now[:hidden_size]
        gate_keep = gate_now[hidden_size:2 * hidden_size]
        candidate = gate_now[2 * hidden_size:3 * hidden_size]
        gate_out = gate_now[3 * hidden_size:]
        squash = jnp.tanh(memory_now)
        grad_memory = grad_memory + grad_state * gate_out * (1.0 - squash * squash)
        grad_summed = jnp.concatenate([grad_memory * candidate * gate_in * (1.0 - gate_in), grad_memory * memory_before * gate_keep * (1.0 - gate_keep), grad_memory * gate_in * (1.0 - candidate * candidate), grad_state * squash * gate_out * (1.0 - gate_out)], axis=0)
        rounded = grad_summed.astype(jnp.bfloat16)
        sum_input = sum_input + lax.dot_general(rounded, inputs_now, contract_cells, preferred_element_type=jnp.float32)
        sum_hidden = sum_hidden + lax.dot_general(rounded, state_before, contract_cells, preferred_element_type=jnp.float32)
        sum_bias = sum_bias + lax.optimization_barrier(jnp.sum(grad_summed, axis=1))
        grad_state = lax.dot_general(hidden_weight, rounded, (((0,), (0,)), ((), ())), preferred_element_type=jnp.float32)
        grad_memory = grad_memory * gate_keep
        return ((grad_state, grad_memory, sum_input, sum_hidden, sum_bias), None)
    start_carry = (grad_hidden, jnp.zeros_like(grad_hidden), jnp.zeros((4 * hidden_size, feat_count), jnp.float32), jnp.zeros((4 * hidden_size, hidden_size), jnp.float32), jnp.zeros((4 * hidden_size,), jnp.float32))
    final_carry, _ = lax.scan(retreat, start_carry, (inputs, gate_values, earlier, memories, states_low), reverse=True)
    return (final_carry[2], final_carry[3], final_carry[4])

def head_params(head_weight, head_offset, hidden):
    act = jnp.dot(head_weight, hidden, precision=lax.Precision.HIGHEST) + head_offset[:, None]
    manning = 0.03 + 0.27 * jax.nn.sigmoid(act[0])
    infiltration = jax.nn.softplus(act[1])
    return jnp.stack([manning, infiltration], axis=0)

def wet_and_out(water_level, infiltration, manning, rainfall, land_frac, root_slope, step_hours):
    wet_depth = land_frac * (water_level + step_hours * rainfall) * jnp.exp(-step_hours * infiltration)
    drain_rate = step_hours * root_slope * (wet_depth + 0.001) ** (2.0 / 3.0) / manning
    return (wet_depth, wet_depth * (1.0 - jnp.exp(-drain_rate)))

def arrivals(padded):
    row_count = padded.shape[1] - 2
    col_count = padded.shape[2]
    framed = jnp.pad(padded, ((0, 0), (0, 0), (1, 1)))
    incoming = jnp.zeros((row_count, col_count), padded.dtype)
    for direction, (row_step, col_step) in enumerate(compass):
        incoming = incoming + framed[direction, 1 - row_step:1 - row_step + row_count, 1 - col_step:1 - col_step + col_count]
    return incoming

def settle(wet_depth, outflow, padded, land_frac):
    return land_frac * (wet_depth - outflow + arrivals(padded))

def fit_term(water_level, observed, land_frac, land_total):
    mismatch = land_frac * (water_level - observed)
    return jnp.sum(mismatch * mismatch) / land_total

def reference(forcing, rainfall, depth_start, observed, land_mask, tile_land, land_rank, flow_code, terrain_slope, input_weight, hidden_weight, gate_bias, head_weight, head_offset):
    land_total = LAND_DEV * N_ROW
    row_count, col_count = depth_start.shape
    cell_count = row_count * col_count
    band_of_row = jnp.arange(row_count, dtype=jnp.int32) // ROWS_DEV
    band_starts = (jnp.cumsum(tile_land) - tile_land).astype(jnp.int32)
    global_rank = jnp.where(land_rank >= 0, land_rank + band_starts[band_of_row][:, None], -1).astype(jnp.int32)
    flat_rank = global_rank.reshape(cell_count)
    target = jnp.where(flat_rank >= 0, flat_rank, land_total).astype(jnp.int32)
    cell_of_rank = jnp.zeros((land_total,), jnp.int32).at[target].set(jnp.arange(cell_count, dtype=jnp.int32), mode='drop')
    flat_forcing = forcing.reshape(SEQ * FEAT, cell_count)

    def block_inputs(block):
        chosen = lax.dynamic_slice_in_dim(cell_of_rank, block * LAND_DEV, LAND_DEV)
        return jnp.take(flat_forcing, chosen, axis=1).reshape(SEQ, FEAT, LAND_DEV)

    def forward_block(carry, block):
        hidden, _ = cell_forward(input_weight, hidden_weight, gate_bias, block_inputs(block))
        return (carry, head_params(head_weight, head_offset, hidden))
    blocks = jnp.arange(N_ROW, dtype=jnp.int32)
    _, stacked = lax.scan(forward_block, jnp.zeros((), jnp.float32), blocks)
    cell_params = jnp.transpose(stacked, (1, 0, 2)).reshape(2, land_total)
    gather_index = jnp.where(flat_rank >= 0, flat_rank, 0).astype(jnp.int32)
    land_frac = land_mask.astype(jnp.float32)
    direction_mask = (flow_code[None] == jnp.arange(8, dtype=jnp.int32)[:, None, None]).astype(jnp.float32)
    root_slope = jnp.sqrt(terrain_slope)
    step_hours = 1.0 / SUB

    def physics(params):
        picked = jnp.take(params, gather_index, axis=1).reshape(2, row_count, col_count)
        manning = jnp.where(land_mask == 1, picked[0], 0.1)
        infiltration = jnp.where(land_mask == 1, picked[1], 1.0)
        water_level = depth_start
        for substep in range(SUB):
            wet_depth, outflow = wet_and_out(water_level, infiltration, manning, rainfall, land_frac, root_slope, step_hours)
            padded = jnp.pad(outflow[None] * direction_mask, ((0, 0), (1, 1), (0, 0)))
            water_level = settle(wet_depth, outflow, padded, land_frac)
        return (fit_term(water_level, observed, land_frac, land_total), water_level)
    misfit, pullback, depth_final = jax.vjp(physics, cell_params, has_aux=True)
    param_grads, = pullback(jnp.ones_like(misfit))
    grad_blocks = param_grads.reshape(2, N_ROW, LAND_DEV)

    def backward_block(sums, block):
        inputs_now = block_inputs(block)
        hidden, stash = cell_forward(input_weight, hidden_weight, gate_bias, inputs_now)
        _, head_pull = jax.vjp(head_params, head_weight, head_offset, hidden)
        block_grads = lax.dynamic_index_in_dim(grad_blocks, block, 1, keepdims=False)
        head_part, offset_part, hidden_part = head_pull(block_grads)
        input_part, recur_part, bias_part = cell_backward(hidden_weight, inputs_now, stash, hidden_part)
        return ((sums[0] + input_part, sums[1] + recur_part, sums[2] + bias_part, sums[3] + head_part, sums[4] + offset_part), None)
    start_sums = (jnp.zeros(input_weight.shape, jnp.float32), jnp.zeros(hidden_weight.shape, jnp.float32), jnp.zeros(gate_bias.shape, jnp.float32), jnp.zeros(head_weight.shape, jnp.float32), jnp.zeros(head_offset.shape, jnp.float32))
    sums, _ = lax.scan(backward_block, start_sums, blocks)
    return (depth_final, misfit.reshape(1), sums[0], sums[1], sums[2], sums[3], sums[4])
```

```python
import jax
import jax.numpy as jnp
from jax import lax
from jax.experimental import pallas as pl
from jax.experimental.pallas import tpu as pltpu
from jax.sharding import PartitionSpec as P

SUB = 6
LAND_DEV = 2048
PAD = 16
EXTRA = 16

compass = ((-1, -1), (-1, 0), (-1, 1), (0, -1), (0, 1), (1, -1), (1, 0), (1, 1))


def forward_kernel(x_ref, perm_ref, w_ref, hwt_ref, off_ref, z_ref, c_ref, act_ref, last_ref, h_scr, c_scr):
    t = pl.program_id(0)
    steps = pl.num_programs(0)
    rows, cols = act_ref.shape[1], act_ref.shape[2]
    hid = c_scr.shape[0]
    feat = perm_ref.shape[0] // rows

    @pl.when(t == 0)
    def _():
        h_scr[...] = jnp.zeros_like(h_scr)
        c_scr[...] = jnp.zeros_like(c_scr)

    moved = jnp.dot(perm_ref[...], x_ref[0], preferred_element_type=jnp.float32).astype(jnp.bfloat16)
    weight = w_ref[...]
    row_id = lax.broadcasted_iota(jnp.int32, (PAD, cols), 0)
    ones = jnp.where(row_id < 3, 1.0, 0.0).astype(jnp.bfloat16)
    for r in range(rows):
        span = slice(r * cols, (r + 1) * cols)
        before = c_scr[:, span]
        state = jnp.concatenate([moved[r * feat:(r + 1) * feat], h_scr[:, span], ones], axis=0)
        z_ref[0, :, span] = state
        c_ref[0, :, span] = before
        gates = jnp.tanh(jnp.dot(weight, state, preferred_element_type=jnp.float32))
        t_in = gates[:hid]
        t_keep = gates[hid:2 * hid]
        cand = gates[2 * hid:3 * hid]
        t_out = gates[3 * hid:]
        memory = 0.5 * ((t_keep + 1.0) * before + (t_in + 1.0) * cand)
        twice = (t_out + 1.0) * jnp.tanh(memory)
        c_scr[:, span] = memory
        h_scr[:, span] = twice.astype(jnp.bfloat16)
        last_ref[:, span] = twice

    @pl.when(t == steps - 1)
    def _():
        for r in range(rows):
            span = slice(r * cols, (r + 1) * cols)
            twice = last_ref[:, span]
            for j in range(2):
                act = jnp.sum(twice * hwt_ref[:, j:j + 1], axis=0, keepdims=True)
                act_ref[j, r:r + 1, :] = act + off_ref[0, j]


def shift_rows(value, step):
    return pltpu.roll(value, step % value.shape[0], 0)


def shift_cols(value, step, col_id):
    cols = value.shape[1]
    moved = pltpu.roll(value, step % cols, 1)
    edge = 0 if step > 0 else cols - 1
    return jnp.where(col_id == edge, 0.0, moved)


def water_kernel(land_total, own_ref, up_ref, dn_ref, act_ref, act_up_ref, act_dn_ref, last_ref, depth_ref, gact_ref, extra_ref):
    rows, cols = depth_ref.shape
    hid = last_ref.shape[0]

    def window(up, own, dn, j):
        return jnp.concatenate([up[j], own[j], dn[j]], axis=0)

    start = window(up_ref, own_ref, dn_ref, 0)
    rain = window(up_ref, own_ref, dn_ref, 1)
    observed = window(up_ref, own_ref, dn_ref, 2)
    root_slope = window(up_ref, own_ref, dn_ref, 3)
    code = window(up_ref, own_ref, dn_ref, 4)
    act0 = window(act_up_ref, act_ref, act_dn_ref, 0)
    act1 = window(act_up_ref, act_ref, act_dn_ref, 1)
    is_land = code > 0.5
    land = jnp.where(is_land, 1.0, 0.0)
    sig0 = 0.5 * jnp.tanh(0.5 * act0) + 0.5
    sig1 = 0.5 * jnp.tanh(0.5 * act1) + 0.5
    soft1 = jnp.maximum(act1, 0.0) + jnp.log(1.0 + jnp.exp(-jnp.abs(act1)))
    manning = jnp.where(is_land, 0.03 + 0.27 * sig0, 0.1)
    infil = jnp.where(is_land, soft1, 1.0)
    dt = 1.0 / SUB
    col_id = lax.broadcasted_iota(jnp.int32, code.shape, 1)
    masks = [jnp.where(code == float(d + 1), 1.0, 0.0) for d in range(8)]
    soak = land * jnp.exp(-dt * infil)
    rain_dt = dt * rain
    rate = dt * root_slope / manning

    def arrive(out):
        total = None
        for col_step in (-1, 0, 1):
            part = None
            for d, (rs, cs) in enumerate(compass):
                if cs != col_step:
                    continue
                flow = out * masks[d]
                flow = shift_rows(flow, rs) if rs else flow
                part = flow if part is None else part + flow
            part = shift_cols(part, col_step, col_id) if col_step else part
            total = part if total is None else total + part
        return total

    def collect(grad):
        total = None
        for col_step in (-1, 0, 1):
            base = shift_cols(grad, -col_step, col_id) if col_step else grad
            for d, (rs, cs) in enumerate(compass):
                if cs != col_step:
                    continue
                back = shift_rows(base, -rs) if rs else base
                back = back * masks[d]
                total = back if total is None else total + back
        return total

    level = start
    kept = []
    for _ in range(SUB):
        wet = (level + rain_dt) * soak
        lifted = wet + 0.001
        power = jnp.exp((2.0 / 3.0) * jnp.log(lifted))
        drain = rate * power
        left = jnp.exp(-drain)
        out = wet * (1.0 - left)
        level = land * (wet - out + arrive(out))
        kept.append((wet, lifted, drain, left))
    own = slice(rows, 2 * rows)
    depth_ref[...] = level[own]
    gap = land * (level - observed)
    own_gap = gap[own]
    misfit = jnp.sum(jnp.sum(own_gap * own_gap, axis=1, keepdims=True), axis=0, keepdims=True) * (1.0 / land_total)
    grad = (2.0 / land_total) * land * gap
    g_drain_sum = jnp.zeros_like(grad)
    g_soak_sum = jnp.zeros_like(grad)
    for wet, lifted, drain, left in reversed(kept):
        settled = land * grad
        g_out = collect(settled) - settled
        g_drain = g_out * wet * left * drain
        g_wet = settled + g_out * (1.0 - left) + (2.0 / 3.0) * g_drain / lifted
        g_drain_sum = g_drain_sum + g_drain
        g_soak_sum = g_soak_sum + g_wet * wet
        grad = g_wet * soak
    g_act0 = jnp.where(is_land, -g_drain_sum / manning * (0.27 * sig0 * (1.0 - sig0)), 0.0)[own]
    g_act1 = jnp.where(is_land, -dt * g_soak_sum * sig1, 0.0)[own]
    gact_ref[0] = g_act0
    gact_ref[1] = g_act1
    extra_ref[...] = jnp.zeros_like(extra_ref)
    for j, g in enumerate((g_act0, g_act1)):
        acc = jnp.zeros((hid, cols), jnp.float32)
        for r in range(rows):
            acc = acc + last_ref[:, r * cols:(r + 1) * cols] * g[r:r + 1, :]
        extra_ref[:hid, j:j + 1] = 0.5 * jnp.sum(acc, axis=1, keepdims=True)
        total = jnp.sum(jnp.sum(g, axis=1, keepdims=True), axis=0, keepdims=True)
        extra_ref[hid:hid + 8, j:j + 1] = jnp.broadcast_to(total, (8, 1))
    extra_ref[hid:hid + 8, 2:3] = jnp.broadcast_to(misfit, (8, 1))


def backward_kernel(z_ref, c_ref, w_ref, wback_ref, hwt_ref, gact_ref, extra_ref, grad_ref, gam_scr, gc_scr, acc_scr):
    k = pl.program_id(0)
    steps = pl.num_programs(0)
    rows, cols = gact_ref.shape[1], gact_ref.shape[2]
    hid = c_ref.shape[1]

    @pl.when(k == 0)
    def _():
        acc_scr[...] = jnp.zeros_like(acc_scr)
        gc_scr[...] = jnp.zeros_like(gc_scr)
        for r in range(rows):
            span = slice(r * cols, (r + 1) * cols)
            gam_scr[:, span] = 0.5 * (
                hwt_ref[:, 0:1] * gact_ref[0, r:r + 1, :] + hwt_ref[:, 1:2] * gact_ref[1, r:r + 1, :]
            )

    weight = w_ref[...]
    wback = wback_ref[...]
    for r in range(rows):
        span = slice(r * cols, (r + 1) * cols)
        state = z_ref[0, :, span]
        before = c_ref[0, :, span]
        gates = jnp.tanh(jnp.dot(weight, state, preferred_element_type=jnp.float32))
        t_in = gates[:hid]
        t_keep = gates[hid:2 * hid]
        cand = gates[2 * hid:3 * hid]
        t_out = gates[3 * hid:]
        p_in = t_in + 1.0
        p_keep = t_keep + 1.0
        held = p_keep * before
        fresh = p_in * cand
        squash = jnp.tanh(0.5 * (held + fresh))
        flow = gam_scr[:, span] * (t_out + 1.0)
        grad_c = gc_scr[:, span] + flow * (1.0 - squash * squash)
        e_in = (grad_c * fresh) * (1.0 - t_in)
        e_keep = (grad_c * held) * (1.0 - t_keep)
        e_cand = (grad_c * p_in) * (1.0 - cand * cand)
        e_out = (flow * squash) * (1.0 - t_out)
        gc_scr[:, span] = 0.5 * (grad_c * p_keep)
        low = jnp.concatenate([e_in, e_keep, e_cand, e_out], axis=0).astype(jnp.bfloat16)
        gam_scr[:, span] = jnp.dot(wback, low, preferred_element_type=jnp.float32)
        acc_scr[...] += lax.dot_general(low, state, (((1,), (1,)), ((), ())), preferred_element_type=jnp.float32)

    @pl.when(k == steps - 1)
    def _():
        width = acc_scr.shape[1]
        grad_ref[:, :width] = acc_scr[...]
        grad_ref[:, width:] = extra_ref[...]


def all_sum(value, axis):
    count = lax.axis_size(axis)
    stride = 1
    while stride < count:
        value = value + lax.ppermute(value, axis, [(i, i ^ stride) for i in range(count)])
        stride *= 2
    return value


def neighbours(value):
    count = lax.axis_size("row")
    from_up = lax.ppermute(value, "row", [(i, i + 1) for i in range(count - 1)])
    from_dn = lax.ppermute(value, "row", [(i + 1, i) for i in range(count - 1)])
    return from_up, from_dn


def shards(
    forcing, rainfall, depth_start, observed, land_mask, tile_land, land_rank, flow_code, terrain_slope,
    input_weight, hidden_weight, gate_bias, head_weight, head_offset,
):
    steps, feat, rows, cols = forcing.shape
    hid = hidden_weight.shape[1]
    cells = rows * cols
    depth = feat + hid + PAD
    land_total = LAND_DEV * lax.axis_size("row")
    f32, bf16 = jnp.float32, jnp.bfloat16

    code = jnp.where(land_mask == 1, flow_code + 1, 0).astype(f32)
    fields = jnp.stack([depth_start, rainfall, observed, jnp.sqrt(terrain_slope), code])
    fields_up, fields_dn = neighbours(fields)

    gate = jnp.arange(4 * hid) // hid
    half = jnp.where(gate == 2, 1.0, 0.5)[:, None]
    bias = gate_bias[:, None] * half
    bias_hi = lax.reduce_precision(bias, 8, 7)
    bias_mid = lax.reduce_precision(bias - bias_hi, 8, 7)
    bias_lo = bias - bias_hi - bias_mid
    weight = jnp.concatenate(
        [
            (input_weight.astype(f32) * half).astype(bf16),
            (hidden_weight.astype(f32) * (0.5 * half)).astype(bf16),
            bias_hi.astype(bf16), bias_mid.astype(bf16), bias_lo.astype(bf16),
            jnp.zeros((4 * hid, PAD - 3), bf16),
        ],
        axis=1,
    )
    back_scale = jnp.where(gate < 2, 0.125, 0.25)[:, None]
    wback = (hidden_weight.astype(f32) * back_scale).astype(bf16).T
    hwt = 0.5 * head_weight.T
    place = jnp.arange(feat * rows)
    perm = ((place % feat * rows + place // feat)[:, None] == place[None, :]).astype(bf16)

    whole = lambda *_: (0, 0)
    whole3 = lambda *_: (0, 0, 0)
    z_all, c_all, act, last = pl.pallas_call(
        forward_kernel,
        grid=(steps,),
        in_specs=[
            pl.BlockSpec((1, feat * rows, cols), lambda t: (t, 0, 0)),
            pl.BlockSpec(perm.shape, whole),
            pl.BlockSpec(weight.shape, whole),
            pl.BlockSpec(hwt.shape, whole),
            pl.BlockSpec(memory_space=pltpu.SMEM),
        ],
        out_specs=[
            pl.BlockSpec((1, depth, cells), lambda t: (t, 0, 0)),
            pl.BlockSpec((1, hid, cells), lambda t: (t, 0, 0)),
            pl.BlockSpec((2, rows, cols), whole3),
            pl.BlockSpec((hid, cells), whole),
        ],
        out_shape=[
            jax.ShapeDtypeStruct((steps, depth, cells), bf16),
            jax.ShapeDtypeStruct((steps, hid, cells), f32),
            jax.ShapeDtypeStruct((2, rows, cols), f32),
            jax.ShapeDtypeStruct((hid, cells), f32),
        ],
        scratch_shapes=[pltpu.VMEM((hid, cells), bf16), pltpu.VMEM((hid, cells), f32)],
        compiler_params=pltpu.CompilerParams(vmem_limit_bytes=48 << 20),
    )(forcing.reshape(steps, feat * rows, cols), perm, weight, hwt, head_offset.reshape(1, 2))

    act_up, act_dn = neighbours(act)
    vmem = pl.BlockSpec(memory_space=pltpu.VMEM)

    def water(*refs):
        water_kernel(land_total, *refs)

    depth_final, gact, extra = pl.pallas_call(
        water,
        in_specs=[vmem] * 7,
        out_specs=[vmem] * 3,
        out_shape=[
            jax.ShapeDtypeStruct((rows, cols), f32),
            jax.ShapeDtypeStruct((2, rows, cols), f32),
            jax.ShapeDtypeStruct((4 * hid, EXTRA), f32),
        ],
        compiler_params=pltpu.CompilerParams(vmem_limit_bytes=32 << 20),
    )(fields, fields_up, fields_dn, act, act_up, act_dn, last)

    total_width = depth + EXTRA
    grads = pl.pallas_call(
        backward_kernel,
        grid=(steps,),
        in_specs=[
            pl.BlockSpec((1, depth, cells), lambda k: (steps - 1 - k, 0, 0)),
            pl.BlockSpec((1, hid, cells), lambda k: (steps - 1 - k, 0, 0)),
            pl.BlockSpec(weight.shape, whole),
            pl.BlockSpec(wback.shape, whole),
            pl.BlockSpec(hwt.shape, whole),
            pl.BlockSpec((2, rows, cols), whole3),
            pl.BlockSpec((4 * hid, EXTRA), whole),
        ],
        out_specs=pl.BlockSpec((4 * hid, total_width), whole),
        out_shape=jax.ShapeDtypeStruct((4 * hid, total_width), f32),
        scratch_shapes=[
            pltpu.VMEM((hid, cells), f32),
            pltpu.VMEM((hid, cells), f32),
            pltpu.VMEM((4 * hid, depth), f32),
        ],
        compiler_params=pltpu.CompilerParams(vmem_limit_bytes=48 << 20),
    )(z_all, c_all, weight, wback, hwt, gact, extra)

    total = all_sum(grads, "row")
    true_scale = jnp.where(gate < 2, 0.5, 1.0)[:, None]
    return (
        depth_final,
        total[hid:hid + 1, depth + 2],
        total[:, :feat] * true_scale,
        total[:, feat:feat + hid] * (0.5 * true_scale),
        total[:, feat + hid] * true_scale[:, 0],
        total[:hid, depth:depth + 2].T,
        total[hid, depth:depth + 2],
    )


def solution(mesh):
    return jax.shard_map(
        shards,
        mesh=mesh,
        in_specs=(
            P(None, None, ("groups", "row"), None),
            P(("groups", "row"), None),
            P(("groups", "row"), None),
            P(("groups", "row"), None),
            P("row", None),
            P(),
            P("row", None),
            P("row", None),
            P("row", None),
            P(),
            P(),
            P(),
            P(),
            P(),
        ),
        out_specs=(
            P(("groups", "row"), None),
            P("groups"),
            P("groups", None),
            P("groups", None),
            P("groups"),
            P("groups", None),
            P("groups"),
        ),
        check_vma=False,
    )
```

```python
import jax
import jax.numpy as jnp
from jax import lax
from jax.experimental import pallas as pl
from jax.experimental.pallas import tpu as pltpu
from jax.sharding import PartitionSpec as P

SUB = 6
LAND_DEV = 2048
PAD = 16
HALO = 2 * SUB
FIELDS = 7
GROUP = 8

compass = ((-1, -1), (-1, 0), (-1, 1), (0, -1), (0, 1), (1, -1), (1, 0), (1, 1))


def gate_rows(array, hid):
    return jnp.concatenate(
        [array[q * hid + g:q * hid + g + GROUP] for g in range(0, hid, GROUP) for q in range(4)], axis=0
    )


def row_scale(shape, hid, values):
    row = lax.broadcasted_iota(jnp.int32, shape, 0) % (4 * GROUP) // GROUP
    return jnp.where(row == 0, values[0], jnp.where(row == 1, values[1], jnp.where(row == 2, values[2], values[3])))


def cell_gates(a, g):
    base = 4 * g
    return [jnp.tanh(a[base + q * GROUP:base + (q + 1) * GROUP]) for q in range(4)]


def forward_kernel(
    x_hbm, input_ref, hidden_ref, bias_ref, head_ref, off_ref, mask_ref, flow_ref, slope_ref, start_ref, rain_ref,
    observed_ref, z_hbm, c_hbm, weight_ref, wback_ref, hwt_ref, own_ref, to_dn_ref, to_up_ref, last_ref,
    x_buf, z_buf, c_buf, perm_scr, x_sem, z_sem, c_sem,
):
    steps = x_buf.shape[0]
    rows, cols = start_ref.shape
    feat = input_ref.shape[1]
    hid = hidden_ref.shape[1]
    cells = rows * cols
    depth = feat + hid + PAD
    f32, bf16 = jnp.float32, jnp.bfloat16

    def x_copy(t):
        return pltpu.make_async_copy(x_hbm.at[t], x_buf.at[t], x_sem.at[t])

    def z_copy(t):
        return pltpu.make_async_copy(z_buf.at[t], z_hbm.at[t], z_sem.at[t])

    def c_copy(t):
        return pltpu.make_async_copy(c_buf.at[t], c_hbm.at[t], c_sem.at[t])

    def span(r):
        return slice(r * cols, (r + 1) * cols)

    for t in range(steps):
        x_copy(t).start()

    shape = perm_scr.shape
    place = lax.broadcasted_iota(jnp.int32, shape, 0)
    source = place % feat * rows + place // feat
    perm_scr[...] = jnp.where(source == lax.broadcasted_iota(jnp.int32, shape, 1), 1.0, 0.0).astype(bf16)
    own_ref[2] = start_ref[...]
    own_ref[3] = rain_ref[...]
    own_ref[4] = observed_ref[...]
    own_ref[5] = jnp.sqrt(slope_ref[...])
    own_ref[6] = jnp.where(mask_ref[...] == 1, flow_ref[...] + 1, 0).astype(f32)
    inputs = gate_rows(input_ref[...].astype(f32), hid)
    hidden = gate_rows(hidden_ref[...].astype(f32), hid)
    bias = jnp.broadcast_to(bias_ref[...], (128, 4 * hid)).T
    bias = gate_rows(bias, hid)
    half = (0.5, 0.5, 1.0, 0.5)
    weight_ref[:, :feat] = (inputs * row_scale(inputs.shape, hid, half)).astype(bf16)
    weight_ref[:, feat:feat + hid] = (0.5 * hidden * row_scale(hidden.shape, hid, half)).astype(bf16)
    bias = bias * row_scale(bias.shape, hid, half)
    bias_hi = bias.astype(bf16).astype(f32)
    bias_mid = (bias - bias_hi).astype(bf16).astype(f32)
    bias_lo = bias - bias_hi - bias_mid
    col_id = lax.broadcasted_iota(jnp.int32, bias.shape, 1)
    bias = jnp.where(col_id == 0, bias_hi, jnp.where(col_id == 1, bias_mid, jnp.where(col_id == 2, bias_lo, 0.0)))
    weight_ref[:, feat + hid:] = bias[:, :PAD].astype(bf16)
    back = hidden * row_scale(hidden.shape, hid, (0.125, 0.125, 0.25, 0.25))
    back = jnp.concatenate([back, jnp.zeros((4 * hid, 128 - hid), f32)], axis=1)
    wback_ref[...] = back.T[:hid].astype(bf16)
    head = jnp.concatenate([head_ref[...], jnp.zeros((126, hid), f32)], axis=0)
    head = jnp.concatenate([head, jnp.zeros((128, 128 - hid), f32)], axis=1)
    hwt_ref[...] = 0.5 * head.T[:hid]

    c_buf[0] = jnp.zeros((hid, cells), f32)
    z_buf[0, feat:feat + hid, :] = jnp.zeros((hid, cells), bf16)
    ones = jnp.where(lax.broadcasted_iota(jnp.int32, (PAD, cells), 0) < 3, 1.0, 0.0).astype(bf16)

    def permute(t):
        x_copy(t).wait()
        moved = jnp.dot(perm_scr[...], x_buf[t], preferred_element_type=f32).astype(bf16)
        for r in range(rows):
            z_buf[t, :feat, span(r)] = moved[r * feat:(r + 1) * feat]
        z_buf[t, feat + hid:, :] = ones

    def step(t, final):
        z_copy(t).start()
        c_copy(t).start()
        weight = weight_ref[...]

        def gates(r):
            return jnp.dot(weight, z_buf[t, :, span(r)], preferred_element_type=f32)

        ahead = gates(0)
        for r in range(rows):
            a = ahead
            ahead = gates(r + 1) if r + 1 < rows else None
            if r == rows // 2 and not final:
                permute(t + 1)
            before = c_buf[t, :, span(r)]
            memories, states = [], []
            for g in range(0, hid, GROUP):
                t_in, t_keep, cand, t_out = cell_gates(a, g)
                memory = 0.5 * ((t_keep + 1.0) * before[g:g + GROUP] + (t_in + 1.0) * cand)
                memories.append(memory)
                states.append((t_out + 1.0) * jnp.tanh(memory))
            state = jnp.concatenate(states, axis=0)
            if final:
                last_ref[:, span(r)] = state
                for j in range(2):
                    act = jnp.sum(state * hwt_ref[:, j:j + 1], axis=0, keepdims=True)
                    own_ref[j, r:r + 1, :] = act + off_ref[j]
            else:
                c_buf[t + 1, :, span(r)] = jnp.concatenate(memories, axis=0)
                z_buf[t + 1, feat:feat + hid, span(r)] = state.astype(bf16)

    permute(0)

    def pair(i, carry):
        step(2 * i, False)
        step(2 * i + 1, False)
        return carry

    lax.fori_loop(0, (steps - 2) // 2, pair, 0)
    step(steps - 2, False)
    step(steps - 1, True)
    for j in range(FIELDS):
        to_dn_ref[j * HALO:(j + 1) * HALO, :] = own_ref[j, rows - HALO:, :]
        to_up_ref[j * HALO:(j + 1) * HALO, :] = own_ref[j, :HALO, :]
    for t in range(steps):
        z_copy(t).wait()
        c_copy(t).wait()


def shift_rows(value, step):
    return pltpu.roll(value, step % value.shape[0], 0)


def shift_cols(value, step, col_id):
    cols = value.shape[1]
    moved = pltpu.roll(value, step % cols, 1)
    edge = 0 if step > 0 else cols - 1
    return jnp.where(col_id == edge, 0.0, moved)


def water_kernel(land_total, own_ref, up_ref, dn_ref, last_ref, depth_ref, gact_ref, extra_ref):
    rows, cols = depth_ref.shape
    hid = last_ref.shape[0]
    spare = jnp.zeros((rows - HALO, cols), jnp.float32)

    def window(j):
        halo = slice(j * HALO, (j + 1) * HALO)
        return jnp.concatenate([spare, up_ref[halo], own_ref[j], dn_ref[halo], spare], axis=0)

    act0, act1, start, rain, observed, root_slope, code = [window(j) for j in range(FIELDS)]
    is_land = code > 0.5
    land = jnp.where(is_land, 1.0, 0.0)
    sig0 = 0.5 * jnp.tanh(0.5 * act0) + 0.5
    sig1 = 0.5 * jnp.tanh(0.5 * act1) + 0.5
    soft1 = jnp.maximum(act1, 0.0) + jnp.log(1.0 + jnp.exp(-jnp.abs(act1)))
    manning = jnp.where(is_land, 0.03 + 0.27 * sig0, 0.1)
    infil = jnp.where(is_land, soft1, 1.0)
    dt = 1.0 / SUB
    col_id = lax.broadcasted_iota(jnp.int32, code.shape, 1)
    masks = [jnp.where(code == float(d + 1), 1.0, 0.0) for d in range(8)]
    soak = land * jnp.exp(-dt * infil)
    rain_dt = dt * rain
    rate = dt * root_slope / manning

    def arrive(out):
        total = None
        for col_step in (-1, 0, 1):
            part = None
            for d, (rs, cs) in enumerate(compass):
                if cs != col_step:
                    continue
                flow = out * masks[d]
                flow = shift_rows(flow, rs) if rs else flow
                part = flow if part is None else part + flow
            part = shift_cols(part, col_step, col_id) if col_step else part
            total = part if total is None else total + part
        return total

    def collect(grad):
        total = None
        for col_step in (-1, 0, 1):
            base = shift_cols(grad, -col_step, col_id) if col_step else grad
            for d, (rs, cs) in enumerate(compass):
                if cs != col_step:
                    continue
                back = shift_rows(base, -rs) if rs else base
                back = back * masks[d]
                total = back if total is None else total + back
        return total

    level = start
    kept = []
    for _ in range(SUB):
        wet = (level + rain_dt) * soak
        lifted = wet + 0.001
        power = jnp.exp((2.0 / 3.0) * jnp.log(lifted))
        drain = rate * power
        left = jnp.exp(-drain)
        out = wet * (1.0 - left)
        level = land * (wet - out + arrive(out))
        kept.append((wet, lifted, drain, left))
    own = slice(rows, 2 * rows)
    depth_ref[...] = level[own]
    gap = land * (level - observed)
    own_gap = gap[own]
    misfit = jnp.sum(jnp.sum(own_gap * own_gap, axis=1, keepdims=True), axis=0, keepdims=True) * (1.0 / land_total)
    grad = (2.0 / land_total) * land * gap
    g_drain_sum = jnp.zeros_like(grad)
    g_soak_sum = jnp.zeros_like(grad)
    for wet, lifted, drain, left in reversed(kept):
        settled = land * grad
        g_out = collect(settled) - settled
        g_drain = g_out * wet * left * drain
        g_wet = settled + g_out * (1.0 - left) + (2.0 / 3.0) * g_drain / lifted
        g_drain_sum = g_drain_sum + g_drain
        g_soak_sum = g_soak_sum + g_wet * wet
        grad = g_wet * soak
    g_act0 = jnp.where(is_land, -g_drain_sum / manning * (0.27 * sig0 * (1.0 - sig0)), 0.0)[own]
    g_act1 = jnp.where(is_land, -dt * g_soak_sum * sig1, 0.0)[own]
    gact_ref[0] = g_act0
    gact_ref[1] = g_act1
    sums, totals = [], []
    for g in (g_act0, g_act1):
        acc = jnp.zeros((hid, cols), jnp.float32)
        for r in range(rows):
            acc = acc + last_ref[:, r * cols:(r + 1) * cols] * g[r:r + 1, :]
        sums.append(acc)
        totals.append(jnp.sum(jnp.sum(g, axis=1, keepdims=True), axis=0, keepdims=True))
    heads = 0.5 * jnp.sum(jnp.concatenate(sums, axis=0).T, axis=0, keepdims=True)
    lane = lax.broadcasted_iota(jnp.int32, heads.shape, 1)
    rest = jnp.where(lane == 0, totals[0], jnp.where(lane == 1, totals[1], jnp.where(lane == 2, misfit, 0.0)))
    line = jnp.concatenate([heads, rest], axis=1)
    row = lax.broadcasted_iota(jnp.int32, extra_ref.shape, 0)
    extra_ref[...] = jnp.where(row == 1, line, 0.0)


def backward_kernel(
    side_ref, z_ref, c_ref, weight_ref, wback_ref, hwt_ref, gact_ref, extra_ref, keep_ref, send_ref, gam_scr, gc_scr, acc_scr
):
    k = pl.program_id(0)
    trips = pl.num_programs(0)
    rows, cols = gact_ref.shape[1], gact_ref.shape[2]
    unroll, hid = c_ref.shape[0], c_ref.shape[1]

    def span(r):
        return slice(r * cols, (r + 1) * cols)

    @pl.when(k == 0)
    def _():
        acc_scr[...] = jnp.zeros_like(acc_scr)
        gc_scr[...] = jnp.zeros_like(gc_scr)
        for r in range(rows):
            gam_scr[:, span(r)] = 0.5 * (
                hwt_ref[:, 0:1] * gact_ref[0, r:r + 1, :] + hwt_ref[:, 1:2] * gact_ref[1, r:r + 1, :]
            )

    weight = weight_ref[...]
    wback = wback_ref[...]
    order = [(u, r) for u in range(unroll - 1, -1, -1) for r in range(rows)]

    def gates(u, r):
        return jnp.dot(weight, z_ref[u, :, span(r)], preferred_element_type=jnp.float32)

    def spread(u, r, low):
        gam_scr[:, span(r)] = jnp.dot(wback, low, preferred_element_type=jnp.float32)
        acc_scr[...] += lax.dot_general(
            z_ref[u, :, span(r)], low, (((1,), (1,)), ((), ())), preferred_element_type=jnp.float32
        )

    ahead = gates(*order[0])
    low = None
    for i, (u, r) in enumerate(order):
        a = ahead
        ahead = gates(*order[i + 1]) if i + 1 < len(order) else None
        if low is not None:
            spread(*order[i - 1], low)
        before = c_ref[u, :, span(r)]
        gam = gam_scr[:, span(r)]
        carried = gc_scr[:, span(r)]
        lows, passed = [], []
        for g in range(0, hid, GROUP):
            part = slice(g, g + GROUP)
            t_in, t_keep, cand, t_out = cell_gates(a, g)
            p_in = t_in + 1.0
            p_keep = t_keep + 1.0
            held = p_keep * before[part]
            fresh = p_in * cand
            squash = jnp.tanh(0.5 * (held + fresh))
            flow = gam[part] * (t_out + 1.0)
            grad_c = carried[part] + flow * (1.0 - squash * squash)
            e_in = (grad_c * fresh) * (1.0 - t_in)
            e_keep = (grad_c * held) * (1.0 - t_keep)
            e_cand = (grad_c * p_in) * (1.0 - cand * cand)
            e_out = (flow * squash) * (1.0 - t_out)
            passed.append(0.5 * (grad_c * p_keep))
            lows.append(jnp.concatenate([e_in, e_keep, e_cand, e_out], axis=0).astype(jnp.bfloat16))
        gc_scr[:, span(r)] = jnp.concatenate(passed, axis=0)
        low = jnp.concatenate(lows, axis=0)
    spread(*order[-1], low)

    @pl.when(k == trips - 1)
    def _():
        used = keep_ref.shape[0] - 8
        whole = jnp.concatenate([acc_scr[:used], extra_ref[...]], axis=0)
        row = lax.broadcasted_iota(jnp.int32, whole.shape, 0)
        whole = jnp.where(row == used, acc_scr[used:used + 1], whole)
        half = whole.shape[1] // 2
        left, right = whole[:, :half], whole[:, half:]
        first = side_ref[0] == 0
        keep_ref[...] = jnp.where(first, left, right)
        send_ref[...] = jnp.where(first, right, left)


def finish_kernel(feat, side_ref, mine_ref, other_ref, input_ref, hidden_ref, bias_ref, head_ref, offset_ref, misfit_ref):
    hid = hidden_ref.shape[1]
    mine, other = mine_ref[...], other_ref[...]
    first = side_ref[0] == 0
    left = jnp.where(first, mine, other)
    right = jnp.where(first, other, mine)
    whole = jnp.concatenate([left, right], axis=1)
    row = feat + hid + 1
    extra = whole[row:row + 1]
    whole = jnp.concatenate([whole, jnp.zeros((128 - whole.shape[0], 4 * hid), jnp.float32)], axis=0)
    turned = whole.T
    turned = turned * row_scale(turned.shape, hid, (0.5, 0.5, 1.0, 1.0))
    turned = jnp.concatenate(
        [turned[4 * g + q * GROUP:4 * g + (q + 1) * GROUP] for q in range(4) for g in range(0, hid, GROUP)], axis=0
    )
    input_ref[...] = turned[:, :feat]
    hidden_ref[...] = 0.5 * turned[:, feat:feat + hid]
    bias_ref[...] = turned.T[feat + hid:feat + hid + 1]
    head_ref[0:1, :] = extra[:, :hid]
    head_ref[1:2, :] = extra[:, hid:2 * hid]
    offset_ref[...] = extra[:, 2 * hid:2 * hid + 2]
    misfit_ref[...] = extra[:, 2 * hid + 2:2 * hid + 3]


def swap(value, stride):
    count = lax.axis_size("row")
    return lax.ppermute(value, "row", [(i, i ^ stride) for i in range(count)])


def shards(
    forcing, rainfall, depth_start, observed, land_mask, tile_land, land_rank, flow_code, terrain_slope,
    input_weight, hidden_weight, gate_bias, head_weight, head_offset,
):
    steps, feat, rows, cols = forcing.shape
    hid = hidden_weight.shape[1]
    cells = rows * cols
    depth = feat + hid + PAD
    payload = feat + hid + 8
    count = lax.axis_size("row")
    land_total = LAND_DEV * count
    f32, bf16 = jnp.float32, jnp.bfloat16
    vmem = pl.BlockSpec(memory_space=pltpu.VMEM)
    smem = pl.BlockSpec(memory_space=pltpu.SMEM)
    hbm = pl.BlockSpec(memory_space=pl.ANY)
    shape = jax.ShapeDtypeStruct

    z_all, c_all, weight, wback, hwt, own, to_dn, to_up, last = pl.pallas_call(
        forward_kernel,
        in_specs=[hbm] + [vmem] * 4 + [smem] + [vmem] * 6,
        out_specs=[hbm] * 2 + [vmem] * 7,
        out_shape=[
            shape((steps, depth, cells), bf16),
            shape((steps, hid, cells), f32),
            shape((4 * hid, depth), bf16),
            shape((hid, 4 * hid), bf16),
            shape((hid, 128), f32),
            shape((FIELDS, rows, cols), f32),
            shape((FIELDS * HALO, cols), f32),
            shape((FIELDS * HALO, cols), f32),
            shape((hid, cells), f32),
        ],
        scratch_shapes=[
            pltpu.VMEM((steps, feat * rows, cols), bf16),
            pltpu.VMEM((steps, depth, cells), bf16),
            pltpu.VMEM((steps, hid, cells), f32),
            pltpu.VMEM((feat * rows, feat * rows), bf16),
            pltpu.SemaphoreType.DMA((steps,)),
            pltpu.SemaphoreType.DMA((steps,)),
            pltpu.SemaphoreType.DMA((steps,)),
        ],
        compiler_params=pltpu.CompilerParams(vmem_limit_bytes=56 << 20),
    )(
        forcing.reshape(steps, feat * rows, cols), input_weight, hidden_weight, gate_bias.reshape(1, 4 * hid),
        head_weight, head_offset, land_mask, flow_code, terrain_slope, depth_start, rainfall, observed,
    )

    from_up = lax.ppermute(to_dn, "row", [(i, i + 1) for i in range(count - 1)])
    from_dn = lax.ppermute(to_up, "row", [(i + 1, i) for i in range(count - 1)])

    def water(*refs):
        water_kernel(land_total, *refs)

    depth_final, gact, extra = pl.pallas_call(
        water,
        in_specs=[vmem] * 4,
        out_specs=[vmem] * 3,
        out_shape=[shape((rows, cols), f32), shape((2, rows, cols), f32), shape((8, 4 * hid), f32)],
        compiler_params=pltpu.CompilerParams(vmem_limit_bytes=32 << 20),
    )(own, from_up, from_dn, last)

    side = (lax.axis_index("row") % 2).astype(jnp.int32).reshape(1)
    unroll = 2
    trips = steps // unroll
    fixed = lambda k: (0, 0)
    keep, send = pl.pallas_call(
        backward_kernel,
        grid=(trips,),
        in_specs=[
            smem,
            pl.BlockSpec((unroll, depth, cells), lambda k: (trips - 1 - k, 0, 0)),
            pl.BlockSpec((unroll, hid, cells), lambda k: (trips - 1 - k, 0, 0)),
            pl.BlockSpec(weight.shape, fixed),
            pl.BlockSpec(wback.shape, fixed),
            pl.BlockSpec(hwt.shape, fixed),
            pl.BlockSpec((2, rows, cols), lambda k: (0, 0, 0)),
            pl.BlockSpec(extra.shape, fixed),
        ],
        out_specs=[pl.BlockSpec((payload, 2 * hid), fixed)] * 2,
        out_shape=[shape((payload, 2 * hid), f32)] * 2,
        scratch_shapes=[
            pltpu.VMEM((hid, cells), f32),
            pltpu.VMEM((hid, cells), f32),
            pltpu.VMEM((depth, 4 * hid), f32),
        ],
        compiler_params=pltpu.CompilerParams(vmem_limit_bytes=56 << 20),
    )(side, z_all, c_all, weight, wback, hwt, gact, extra)

    mine = keep + swap(send, 1)
    stride = 2
    while stride < count:
        mine = mine + swap(mine, stride)
        stride *= 2
    other = swap(mine, 1)

    def finish(*refs):
        finish_kernel(feat, *refs)

    grads = pl.pallas_call(
        finish,
        in_specs=[smem, vmem, vmem],
        out_specs=[vmem] * 6,
        out_shape=[
            shape((4 * hid, feat), f32),
            shape((4 * hid, hid), f32),
            shape((1, 4 * hid), f32),
            shape((2, hid), f32),
            shape((1, 2), f32),
            shape((1, 1), f32),
        ],
    )(side, mine, other)
    return (
        depth_final, grads[5].reshape(1), grads[0], grads[1], grads[2].reshape(4 * hid), grads[3], grads[4].reshape(2),
    )


def solution(mesh):
    return jax.shard_map(
        shards,
        mesh=mesh,
        in_specs=(
            P(None, None, ("groups", "row"), None),
            P(("groups", "row"), None),
            P(("groups", "row"), None),
            P(("groups", "row"), None),
            P("row", None),
            P(),
            P("row", None),
            P("row", None),
            P("row", None),
            P(),
            P(),
            P(),
            P(),
            P(),
        ),
        out_specs=(
            P(("groups", "row"), None),
            P("groups"),
            P("groups", None),
            P("groups", None),
            P("groups"),
            P("groups", None),
            P("groups"),
        ),
        check_vma=False,
    )
```

```python
import jax
import jax.numpy as jnp
from jax import lax
from jax.experimental import pallas as pl
from jax.experimental.pallas import tpu as pltpu
from jax.sharding import PartitionSpec as P

SUB = 6
LAND_DEV = 2048
PAD = 16
HALO = 2 * SUB
FIELDS = 7
GROUP = 8
AHEAD = 1

compass = ((-1, -1), (-1, 0), (-1, 1), (0, -1), (0, 1), (1, -1), (1, 0), (1, 1))


def gate_rows(array, hid):
    return jnp.concatenate(
        [array[q * hid + g:q * hid + g + GROUP] for g in range(0, hid, GROUP) for q in range(4)], axis=0
    )


def row_scale(shape, hid, values):
    row = lax.broadcasted_iota(jnp.int32, shape, 0) % (4 * GROUP) // GROUP
    return jnp.where(row == 0, values[0], jnp.where(row == 1, values[1], jnp.where(row == 2, values[2], values[3])))


def cell_gates(a, g):
    base = 4 * g
    return [jnp.tanh(a[base + q * GROUP:base + (q + 1) * GROUP]) for q in range(4)]


def forward_kernel(
    x_hbm, input_ref, hidden_ref, bias_ref, head_ref, off_ref, mask_ref, flow_ref, slope_ref, start_ref, rain_ref,
    observed_ref, z_hbm, c_hbm, weight_ref, wback_ref, hwt_ref, own_ref, to_dn_ref, to_up_ref, last_ref,
    x_buf, z_buf, c_buf, perm_scr, x_sem, z_sem, c_sem,
):
    steps = x_buf.shape[0]
    rows, cols = start_ref.shape
    feat = input_ref.shape[0]
    hid = hidden_ref.shape[0]
    cells = rows * cols
    depth = feat + hid + PAD
    f32, bf16 = jnp.float32, jnp.bfloat16

    def x_copy(t):
        return pltpu.make_async_copy(x_hbm.at[t], x_buf.at[t], x_sem.at[t])

    def z_copy(t):
        return pltpu.make_async_copy(z_buf.at[t], z_hbm.at[t], z_sem.at[t])

    def c_copy(t):
        return pltpu.make_async_copy(c_buf.at[t], c_hbm.at[t], c_sem.at[t])

    def span(r):
        return slice(r * cols, (r + 1) * cols)

    for t in range(2):
        x_copy(t).start()

    shape = perm_scr.shape
    place = lax.broadcasted_iota(jnp.int32, shape, 0)
    source = place % feat * rows + place // feat
    perm_scr[...] = jnp.where(source == lax.broadcasted_iota(jnp.int32, shape, 1), 1.0, 0.0).astype(bf16)
    own_ref[2] = start_ref[...]
    own_ref[3] = rain_ref[...]
    own_ref[4] = observed_ref[...]
    own_ref[5] = jnp.sqrt(slope_ref[...])
    own_ref[6] = jnp.where(mask_ref[...] == 1, flow_ref[...] + 1, 0).astype(f32)
    bias = jnp.broadcast_to(bias_ref[...], (128 - feat - hid, 4 * hid))
    bias = jnp.where(lax.broadcasted_iota(jnp.int32, bias.shape, 0) < 3, bias, 0.0)
    weight = gate_rows(jnp.concatenate([input_ref[...].astype(f32), hidden_ref[...].astype(f32), bias], axis=0).T, hid)
    col_id = lax.broadcasted_iota(jnp.int32, weight.shape, 1)
    back = jnp.where(col_id < feat + hid, weight, 0.0) * row_scale(weight.shape, hid, (0.125, 0.125, 0.25, 0.25))
    wback_ref[...] = back.T[feat:feat + hid].astype(bf16)
    weight = weight * row_scale(weight.shape, hid, (0.5, 0.5, 1.0, 0.5))
    weight = jnp.where((col_id >= feat) & (col_id < feat + hid), 0.5 * weight, weight)
    high = weight.astype(bf16).astype(f32)
    middle = (weight - high).astype(bf16).astype(f32)
    low = weight - high - middle
    weight = jnp.where(col_id == feat + hid + 1, middle, jnp.where(col_id == feat + hid + 2, low, weight))
    weight_ref[...] = weight[:, :depth].astype(bf16)
    head = jnp.concatenate([head_ref[...], jnp.zeros((126, hid), f32)], axis=0)
    head = jnp.concatenate([head, jnp.zeros((128, 128 - hid), f32)], axis=1)
    hwt_ref[...] = 0.5 * head.T[:hid]

    c_buf[0] = jnp.zeros((hid, cells), f32)
    z_buf[0, feat:feat + hid, :] = jnp.zeros((hid, cells), bf16)
    ones = jnp.where(lax.broadcasted_iota(jnp.int32, (PAD, cells), 0) < 3, 1.0, 0.0).astype(bf16)

    def permute(t):
        x_copy(t).wait()

        @pl.when(t + 2 < steps)
        def _():
            x_copy(t + 2).start()

        moved = jnp.dot(perm_scr[...], x_buf[t], preferred_element_type=f32).astype(bf16)
        for r in range(rows):
            z_buf[t, :feat, span(r)] = moved[r * feat:(r + 1) * feat]
        z_buf[t, feat + hid:, :] = ones

    def step(t, final):
        z_copy(t).start()
        c_copy(t).start()
        weight = weight_ref[...]

        def gates(r):
            return jnp.dot(weight, z_buf[t, :, span(r)], preferred_element_type=f32)

        ahead = gates(0)
        for r in range(rows):
            a = ahead
            ahead = gates(r + 1) if r + 1 < rows else None
            if r == rows // 2 and not final:
                permute(t + 1)
            before = c_buf[t, :, span(r)]
            memories, states = [], []
            for g in range(0, hid, GROUP):
                t_in, t_keep, cand, t_out = cell_gates(a, g)
                memory = 0.5 * ((t_keep + 1.0) * before[g:g + GROUP] + (t_in + 1.0) * cand)
                memories.append(memory)
                states.append((t_out + 1.0) * jnp.tanh(memory))
            state = jnp.concatenate(states, axis=0)
            if final:
                last_ref[:, span(r)] = state
                for j in range(2):
                    act = jnp.sum(state * hwt_ref[:, j:j + 1], axis=0, keepdims=True)
                    own_ref[j, r:r + 1, :] = act + off_ref[j]
            else:
                c_buf[t + 1, :, span(r)] = jnp.concatenate(memories, axis=0)
                z_buf[t + 1, feat:feat + hid, span(r)] = state.astype(bf16)

    permute(0)

    def pair(i, carry):
        step(2 * i, False)
        step(2 * i + 1, False)
        return carry

    lax.fori_loop(0, (steps - 2) // 2, pair, 0)
    step(steps - 2, False)
    step(steps - 1, True)
    for j in range(FIELDS):
        to_dn_ref[j * HALO:(j + 1) * HALO, :] = own_ref[j, rows - HALO:, :]
        to_up_ref[j * HALO:(j + 1) * HALO, :] = own_ref[j, :HALO, :]
    for t in range(steps):
        z_copy(t).wait()
        c_copy(t).wait()


def shift_rows(value, step):
    return pltpu.roll(value, step % value.shape[0], 0)


def shift_cols(value, step, col_id):
    cols = value.shape[1]
    moved = pltpu.roll(value, step % cols, 1)
    edge = 0 if step > 0 else cols - 1
    return jnp.where(col_id == edge, 0.0, moved)


def water(land_total, own_ref, up_ref, dn_ref, depth_ref):
    rows, cols = depth_ref.shape
    spare = jnp.zeros((rows - HALO, cols), jnp.float32)

    def window(j):
        halo = slice(j * HALO, (j + 1) * HALO)
        return jnp.concatenate([spare, up_ref[halo], own_ref[j], dn_ref[halo], spare], axis=0)

    act0, act1, start, rain, observed, root_slope, code = [window(j) for j in range(FIELDS)]
    is_land = code > 0.5
    land = jnp.where(is_land, 1.0, 0.0)
    sig0 = 0.5 * jnp.tanh(0.5 * act0) + 0.5
    sig1 = 0.5 * jnp.tanh(0.5 * act1) + 0.5
    soft1 = jnp.maximum(act1, 0.0) + jnp.log(1.0 + jnp.exp(-jnp.abs(act1)))
    manning = jnp.where(is_land, 0.03 + 0.27 * sig0, 0.1)
    infil = jnp.where(is_land, soft1, 1.0)
    dt = 1.0 / SUB
    col_id = lax.broadcasted_iota(jnp.int32, code.shape, 1)
    masks = [jnp.where(code == float(d + 1), 1.0, 0.0) for d in range(8)]
    soak = land * jnp.exp(-dt * infil)
    rain_dt = dt * rain
    rate = dt * root_slope / manning

    def arrive(out):
        total = None
        for col_step in (-1, 0, 1):
            part = None
            for d, (rs, cs) in enumerate(compass):
                if cs != col_step:
                    continue
                flow = out * masks[d]
                flow = shift_rows(flow, rs) if rs else flow
                part = flow if part is None else part + flow
            part = shift_cols(part, col_step, col_id) if col_step else part
            total = part if total is None else total + part
        return total

    def collect(grad):
        total = None
        for col_step in (-1, 0, 1):
            base = shift_cols(grad, -col_step, col_id) if col_step else grad
            for d, (rs, cs) in enumerate(compass):
                if cs != col_step:
                    continue
                back = shift_rows(base, -rs) if rs else base
                back = back * masks[d]
                total = back if total is None else total + back
        return total

    level = start
    kept = []
    for _ in range(SUB):
        wet = (level + rain_dt) * soak
        lifted = wet + 0.001
        power = jnp.exp((2.0 / 3.0) * jnp.log(lifted))
        drain = rate * power
        left = jnp.exp(-drain)
        out = wet * (1.0 - left)
        level = land * (wet - out + arrive(out))
        kept.append((wet, lifted, drain, left))
    own = slice(rows, 2 * rows)
    depth_ref[...] = level[own]
    gap = land * (level - observed)
    own_gap = gap[own]
    misfit = jnp.sum(jnp.sum(own_gap * own_gap, axis=1, keepdims=True), axis=0, keepdims=True) * (1.0 / land_total)
    grad = (2.0 / land_total) * land * gap
    g_drain_sum = jnp.zeros_like(grad)
    g_soak_sum = jnp.zeros_like(grad)
    for wet, lifted, drain, left in reversed(kept):
        settled = land * grad
        g_out = collect(settled) - settled
        g_drain = g_out * wet * left * drain
        g_wet = settled + g_out * (1.0 - left) + (2.0 / 3.0) * g_drain / lifted
        g_drain_sum = g_drain_sum + g_drain
        g_soak_sum = g_soak_sum + g_wet * wet
        grad = g_wet * soak
    g_act0 = jnp.where(is_land, -g_drain_sum / manning * (0.27 * sig0 * (1.0 - sig0)), 0.0)[own]
    g_act1 = jnp.where(is_land, -dt * g_soak_sum * sig1, 0.0)[own]
    return g_act0, g_act1, misfit


def head_line(last_ref, gact_ref, misfit):
    rows, cols = gact_ref.shape[1], gact_ref.shape[2]
    hid = last_ref.shape[0]
    sums, totals = [], []
    for j in range(2):
        g = gact_ref[j]
        acc = jnp.zeros((hid, cols), jnp.float32)
        for r in range(rows):
            acc = acc + last_ref[:, r * cols:(r + 1) * cols] * g[r:r + 1, :]
        sums.append(acc)
        totals.append(jnp.sum(jnp.sum(g, axis=1, keepdims=True), axis=0, keepdims=True))
    heads = 0.5 * jnp.sum(jnp.concatenate(sums, axis=0).T, axis=0, keepdims=True)
    lane = lax.broadcasted_iota(jnp.int32, heads.shape, 1)
    rest = jnp.where(lane == 0, totals[0], jnp.where(lane == 1, totals[1], jnp.where(lane == 2, misfit, 0.0)))
    return jnp.concatenate([heads, rest], axis=1)


def backward_kernel(
    land_total, unroll, side_ref, z_hbm, c_hbm, weight_hbm, wback_hbm, hwt_hbm, own_hbm, last_hbm, up_ref, dn_ref,
    depth_ref, keep_ref, send_ref, z_buf, c_buf, weight_ref, wback_ref, hwt_ref, own_ref, last_ref, gact_ref,
    gam_scr, gc_scr, acc_scr, z_sem, c_sem, small_sem,
):
    steps, hid = c_buf.shape[0], c_buf.shape[1]
    rows, cols = depth_ref.shape

    def span(r):
        return slice(r * cols, (r + 1) * cols)

    def z_copy(t):
        return pltpu.make_async_copy(z_hbm.at[t], z_buf.at[t], z_sem.at[t])

    def c_copy(t):
        return pltpu.make_async_copy(c_hbm.at[t], c_buf.at[t], c_sem.at[t])

    pairs = (
        (own_hbm, own_ref), (hwt_hbm, hwt_ref), (weight_hbm, weight_ref), (wback_hbm, wback_ref), (last_hbm, last_ref),
    )
    small = [pltpu.make_async_copy(src, dst, small_sem.at[i]) for i, (src, dst) in enumerate(pairs)]
    for copy in small[:4]:
        copy.start()
    for t in range(steps - 1, steps - 1 - AHEAD * unroll, -1):
        z_copy(t).start()
        c_copy(t).start()
        if t == steps - unroll:
            small[4].start()
    acc_scr[...] = jnp.zeros_like(acc_scr)
    gc_scr[...] = jnp.zeros_like(gc_scr)
    small[0].wait()
    g_act0, g_act1, misfit = water(land_total, own_ref, up_ref, dn_ref, depth_ref)
    gact_ref[0] = g_act0
    gact_ref[1] = g_act1
    for copy in small[1:]:
        copy.wait()
    for r in range(rows):
        gam_scr[:, span(r)] = 0.5 * (
            hwt_ref[:, 0:1] * gact_ref[0, r:r + 1, :] + hwt_ref[:, 1:2] * gact_ref[1, r:r + 1, :]
        )
    line = head_line(last_ref, gact_ref, misfit)
    weight = weight_ref[...]
    wback = wback_ref[...]
    order = [(u, r) for u in range(unroll) for r in range(rows)]

    def gates(t, r):
        return jnp.dot(weight, z_buf[t, :, span(r)], preferred_element_type=jnp.float32)

    def spread(t, r, low):
        gam_scr[:, span(r)] = jnp.dot(wback, low, preferred_element_type=jnp.float32)
        acc_scr[...] += lax.dot_general(
            z_buf[t, :, span(r)], low, (((1,), (1,)), ((), ())), preferred_element_type=jnp.float32
        )

    def hours(k, carry):
        top = steps - 1 - unroll * k
        for u in range(unroll):
            later = top - u - AHEAD * unroll

            @pl.when(later >= 0)
            def _(later=later):
                z_copy(later).start()
                c_copy(later).start()

        for u in range(unroll):
            z_copy(top - u).wait()
            c_copy(top - u).wait()
        ahead = gates(top, 0)
        low = None
        for i, (u, r) in enumerate(order):
            a = ahead
            ahead = gates(top - order[i + 1][0], order[i + 1][1]) if i + 1 < len(order) else None
            if low is not None:
                spread(top - order[i - 1][0], order[i - 1][1], low)
            before = c_buf[top - u, :, span(r)]
            gam = gam_scr[:, span(r)]
            carried = gc_scr[:, span(r)]
            lows, passed = [], []
            for g in range(0, hid, GROUP):
                part = slice(g, g + GROUP)
                t_in, t_keep, cand, t_out = cell_gates(a, g)
                p_in = t_in + 1.0
                p_keep = t_keep + 1.0
                held = p_keep * before[part]
                fresh = p_in * cand
                squash = jnp.tanh(0.5 * (held + fresh))
                flow = gam[part] * (t_out + 1.0)
                grad_c = carried[part] + flow * (1.0 - squash * squash)
                e_in = (grad_c * fresh) * (1.0 - t_in)
                e_keep = (grad_c * held) * (1.0 - t_keep)
                e_cand = (grad_c * p_in) * (1.0 - cand * cand)
                e_out = (flow * squash) * (1.0 - t_out)
                passed.append(0.5 * (grad_c * p_keep))
                lows.append(jnp.concatenate([e_in, e_keep, e_cand, e_out], axis=0).astype(jnp.bfloat16))
            gc_scr[:, span(r)] = jnp.concatenate(passed, axis=0)
            low = jnp.concatenate(lows, axis=0)
        spread(top - order[-1][0], order[-1][1], low)
        return carry

    lax.fori_loop(0, steps // unroll, hours, 0)
    used = keep_ref.shape[0] - 8
    row = lax.broadcasted_iota(jnp.int32, (8, 4 * hid), 0)
    extra = jnp.where(row == 0, acc_scr[used:used + 1], jnp.where(row == 1, line, 0.0))
    whole = jnp.concatenate([acc_scr[:used], extra], axis=0)
    half = whole.shape[1] // 2
    left, right = whole[:, :half], whole[:, half:]
    first = side_ref[0] == 0
    keep_ref[...] = jnp.where(first, left, right)
    send_ref[...] = jnp.where(first, right, left)


def finish_kernel(feat, side_ref, mine_ref, other_ref, input_ref, hidden_ref, bias_ref, head_ref, offset_ref, misfit_ref):
    hid = hidden_ref.shape[0]
    mine, other = mine_ref[...], other_ref[...]
    first = side_ref[0] == 0
    left = jnp.where(first, mine, other)
    right = jnp.where(first, other, mine)
    whole = jnp.concatenate([left, right], axis=1)
    row = feat + hid + 1
    extra = whole[row:row + 1]
    whole = jnp.concatenate([whole, jnp.zeros((128 - whole.shape[0], 4 * hid), jnp.float32)], axis=0)
    turned = whole.T
    turned = turned * row_scale(turned.shape, hid, (0.5, 0.5, 1.0, 1.0))
    turned = jnp.concatenate(
        [turned[4 * g + q * GROUP:4 * g + (q + 1) * GROUP] for q in range(4) for g in range(0, hid, GROUP)], axis=0
    )
    turned = turned.T
    input_ref[...] = turned[:feat]
    hidden_ref[...] = 0.5 * turned[feat:feat + hid]
    bias_ref[...] = turned[feat + hid:feat + hid + 1]
    head_ref[0:1, :] = extra[:, :hid]
    head_ref[1:2, :] = extra[:, hid:2 * hid]
    offset_ref[...] = extra[:, 2 * hid:2 * hid + 2]
    misfit_ref[...] = extra[:, 2 * hid + 2:2 * hid + 3]


def swap(value, stride):
    count = lax.axis_size("row")
    return lax.ppermute(value, "row", [(i, i ^ stride) for i in range(count)])


def shards(
    forcing, rainfall, depth_start, observed, land_mask, tile_land, land_rank, flow_code, terrain_slope,
    input_weight, hidden_weight, gate_bias, head_weight, head_offset,
):
    steps, feat, rows, cols = forcing.shape
    hid = hidden_weight.shape[1]
    cells = rows * cols
    depth = feat + hid + PAD
    payload = feat + hid + 8
    count = lax.axis_size("row")
    land_total = LAND_DEV * count
    f32, bf16 = jnp.float32, jnp.bfloat16
    vmem = pl.BlockSpec(memory_space=pltpu.VMEM)
    smem = pl.BlockSpec(memory_space=pltpu.SMEM)
    hbm = pl.BlockSpec(memory_space=pl.ANY)
    shape = jax.ShapeDtypeStruct

    z_all, c_all, weight, wback, hwt, own, to_dn, to_up, last = pl.pallas_call(
        forward_kernel,
        in_specs=[hbm] + [vmem] * 4 + [smem] + [vmem] * 6,
        out_specs=[hbm] * 2 + [vmem] * 7,
        out_shape=[
            shape((steps, depth, cells), bf16),
            shape((steps, hid, cells), f32),
            shape((4 * hid, depth), bf16),
            shape((hid, 4 * hid), bf16),
            shape((hid, 128), f32),
            shape((FIELDS, rows, cols), f32),
            shape((FIELDS * HALO, cols), f32),
            shape((FIELDS * HALO, cols), f32),
            shape((hid, cells), f32),
        ],
        scratch_shapes=[
            pltpu.VMEM((steps, feat * rows, cols), bf16),
            pltpu.VMEM((steps, depth, cells), bf16),
            pltpu.VMEM((steps, hid, cells), f32),
            pltpu.VMEM((feat * rows, feat * rows), bf16),
            pltpu.SemaphoreType.DMA((steps,)),
            pltpu.SemaphoreType.DMA((steps,)),
            pltpu.SemaphoreType.DMA((steps,)),
        ],
        compiler_params=pltpu.CompilerParams(vmem_limit_bytes=56 << 20),
    )(
        forcing.reshape(steps, feat * rows, cols), input_weight.T, hidden_weight.T, gate_bias.reshape(1, 4 * hid),
        head_weight, head_offset, land_mask, flow_code, terrain_slope, depth_start, rainfall, observed,
    )

    from_up = lax.ppermute(to_dn, "row", [(i, i + 1) for i in range(count - 1)])
    from_dn = lax.ppermute(to_up, "row", [(i + 1, i) for i in range(count - 1)])

    side = (lax.axis_index("row") % 2).astype(jnp.int32).reshape(1)
    def backward(*refs):
        backward_kernel(land_total, 2, *refs)

    depth_final, keep, send = pl.pallas_call(
        backward,
        in_specs=[smem] + [hbm] * 7 + [vmem] * 2,
        out_specs=[vmem] * 3,
        out_shape=[shape((rows, cols), f32), shape((payload, 2 * hid), f32), shape((payload, 2 * hid), f32)],
        scratch_shapes=[
            pltpu.VMEM((steps, depth, cells), bf16),
            pltpu.VMEM((steps, hid, cells), f32),
            pltpu.VMEM((4 * hid, depth), bf16),
            pltpu.VMEM((hid, 4 * hid), bf16),
            pltpu.VMEM((hid, 128), f32),
            pltpu.VMEM((FIELDS, rows, cols), f32),
            pltpu.VMEM((hid, cells), f32),
            pltpu.VMEM((2, rows, cols), f32),
            pltpu.VMEM((hid, cells), f32),
            pltpu.VMEM((hid, cells), f32),
            pltpu.VMEM((depth, 4 * hid), f32),
            pltpu.SemaphoreType.DMA((steps,)),
            pltpu.SemaphoreType.DMA((steps,)),
            pltpu.SemaphoreType.DMA((5,)),
        ],
        compiler_params=pltpu.CompilerParams(vmem_limit_bytes=56 << 20),
    )(side, z_all, c_all, weight, wback, hwt, own, last, from_up, from_dn)

    mine = keep + swap(send, 1)
    stride = 2
    while stride < count:
        mine = mine + swap(mine, stride)
        stride *= 2
    other = swap(mine, 1)

    def finish(*refs):
        finish_kernel(feat, *refs)

    grads = pl.pallas_call(
        finish,
        in_specs=[smem, vmem, vmem],
        out_specs=[vmem] * 6,
        out_shape=[
            shape((feat, 4 * hid), f32),
            shape((hid, 4 * hid), f32),
            shape((1, 4 * hid), f32),
            shape((2, hid), f32),
            shape((1, 2), f32),
            shape((1, 1), f32),
        ],
    )(side, mine, other)
    return (
        depth_final, grads[5].reshape(1), grads[0].T, grads[1].T, grads[2].reshape(4 * hid), grads[3], grads[4].reshape(2),
    )


def solution(mesh):
    return jax.shard_map(
        shards,
        mesh=mesh,
        in_specs=(
            P(None, None, ("groups", "row"), None),
            P(("groups", "row"), None),
            P(("groups", "row"), None),
            P(("groups", "row"), None),
            P("row", None),
            P(),
            P("row", None),
            P("row", None),
            P("row", None),
            P(),
            P(),
            P(),
            P(),
            P(),
        ),
        out_specs=(
            P(("groups", "row"), None),
            P("groups"),
            P("groups", None),
            P("groups", None),
            P("groups"),
            P("groups", None),
            P("groups"),
        ),
        check_vma=False,
    )
```

```python
import jax
import jax.numpy as jnp
from jax import lax
from jax.experimental import pallas as pl
from jax.experimental.pallas import tpu as pltpu
from jax.sharding import PartitionSpec as P

SUB = 6
LAND_DEV = 2048
PAD = 16
HALO = 2 * SUB
FIELDS = 7
GROUP = 8
AHEAD = 1
FORWARD_UNROLL = 2
INS = 10
OUTS = 7

compass = ((-1, -1), (-1, 0), (-1, 1), (0, -1), (0, 1), (1, -1), (1, 0), (1, 1))


def gate_rows(array, hid):
    return jnp.concatenate(
        [array[q * hid + g:q * hid + g + GROUP] for g in range(0, hid, GROUP) for q in range(4)], axis=0
    )


def row_scale(shape, hid, values):
    row = lax.broadcasted_iota(jnp.int32, shape, 0) % (4 * GROUP) // GROUP
    return jnp.where(row == 0, values[0], jnp.where(row == 1, values[1], jnp.where(row == 2, values[2], values[3])))


def cell_gates(a, g):
    base = 4 * g
    return [jnp.tanh(a[base + q * GROUP:base + (q + 1) * GROUP]) for q in range(4)]


def forward_kernel(x_hbm, off_ref, *refs):
    in_hbm, (z_hbm, c_hbm), out_hbm = refs[:INS], refs[INS:INS + 2], refs[INS + 2:INS + 2 + OUTS]
    in_buf, out_buf = refs[INS + 2 + OUTS:2 * INS + 2 + OUTS], refs[2 * INS + 2 + OUTS:2 * INS + 2 + 2 * OUTS]
    x_buf, z_buf, c_buf, perm_scr, x_sem, z_sem, c_sem, in_sem, out_sem = refs[2 * INS + 2 + 2 * OUTS:]
    input_ref, hidden_ref, bias_ref, head_ref, mask_ref, flow_ref, slope_ref, start_ref, rain_ref, observed_ref = in_buf
    weight_ref, wback_ref, hwt_ref, own_ref, to_dn_ref, to_up_ref, last_ref = out_buf
    steps = x_buf.shape[0]
    rows, cols = start_ref.shape
    feat = input_ref.shape[0]
    hid = hidden_ref.shape[0]
    cells = rows * cols
    depth = feat + hid + PAD
    f32, bf16 = jnp.float32, jnp.bfloat16
    ins = [pltpu.make_async_copy(in_hbm[i], in_buf[i], in_sem.at[i]) for i in range(INS)]
    outs = [pltpu.make_async_copy(out_buf[i], out_hbm[i], out_sem.at[i]) for i in range(OUTS)]
    for copy in ins:
        copy.start()

    def x_copy(t):
        return pltpu.make_async_copy(x_hbm.at[t], x_buf.at[t], x_sem.at[t])

    def z_copy(t):
        return pltpu.make_async_copy(z_buf.at[t], z_hbm.at[t], z_sem.at[t])

    def c_copy(t):
        return pltpu.make_async_copy(c_buf.at[t], c_hbm.at[t], c_sem.at[t])

    def span(r):
        return slice(r * cols, (r + 1) * cols)

    for t in range(3):
        x_copy(t).start()

    shape = perm_scr.shape
    place = lax.broadcasted_iota(jnp.int32, (shape[0], 1), 0)
    source = place % feat * rows + place // feat
    perm_scr[...] = jnp.where(source == lax.broadcasted_iota(jnp.int32, shape, 1), 1.0, 0.0).astype(bf16)
    for copy in ins:
        copy.wait()
    own_ref[2] = start_ref[...]
    own_ref[3] = rain_ref[...]
    own_ref[4] = observed_ref[...]
    own_ref[5] = jnp.sqrt(slope_ref[...])
    own_ref[6] = jnp.where(mask_ref[...] == 1, flow_ref[...] + 1, 0).astype(f32)
    bias = jnp.broadcast_to(bias_ref[...], (128 - feat - hid, 4 * hid))
    bias = jnp.where(lax.broadcasted_iota(jnp.int32, bias.shape, 0) < 3, bias, 0.0)
    weight = gate_rows(jnp.concatenate([input_ref[...].astype(f32), hidden_ref[...].astype(f32), bias], axis=0).T, hid)
    col_id = lax.broadcasted_iota(jnp.int32, weight.shape, 1)
    back = jnp.where(col_id < feat + hid, weight, 0.0) * row_scale(weight.shape, hid, (0.125, 0.125, 0.25, 0.25))
    wback_ref[...] = back.T[feat:feat + hid].astype(bf16)
    weight = weight * row_scale(weight.shape, hid, (0.5, 0.5, 1.0, 0.5))
    weight = jnp.where((col_id >= feat) & (col_id < feat + hid), 0.5 * weight, weight)
    high = weight.astype(bf16).astype(f32)
    middle = (weight - high).astype(bf16).astype(f32)
    low = weight - high - middle
    weight = jnp.where(col_id == feat + hid + 1, middle, jnp.where(col_id == feat + hid + 2, low, weight))
    weight_ref[...] = weight[:, :depth].astype(bf16)
    head = jnp.concatenate([head_ref[...], jnp.zeros((126, hid), f32)], axis=0)
    head = jnp.concatenate([head, jnp.zeros((128, 128 - hid), f32)], axis=1)
    hwt_ref[...] = 0.5 * head.T[:hid]

    for copy in outs[:3]:
        copy.start()
    c_buf[0] = jnp.zeros((hid, cells), f32)
    z_buf[0, feat:feat + hid, :] = jnp.zeros((hid, cells), bf16)
    ones = jnp.where(lax.broadcasted_iota(jnp.int32, (PAD, cells), 0) < 3, 1.0, 0.0).astype(bf16)

    def permute(t):
        moved = jnp.dot(perm_scr[...], x_buf[jnp.minimum(t, steps - 1)], preferred_element_type=f32).astype(bf16)
        for r in range(rows):
            z_buf[t, :feat, span(r)] = moved[r * feat:(r + 1) * feat]
        z_buf[t, feat + hid:, :] = ones

    def step(t):
        weight = weight_ref[...]

        def gates(r):
            return jnp.dot(weight, z_buf[t, :, span(r)], preferred_element_type=f32)

        ahead = gates(0)
        for r in range(rows):
            a = ahead
            ahead = gates(r + 1) if r + 1 < rows else None
            if r == rows // 2:
                permute(t + 1)
            before = c_buf[t, :, span(r)]
            memories, states = [], []
            for g in range(0, hid, GROUP):
                t_in, t_keep, cand, t_out = cell_gates(a, g)
                memory = 0.5 * ((t_keep + 1.0) * before[g:g + GROUP] + (t_in + 1.0) * cand)
                memories.append(memory)
                states.append((t_out + 1.0) * jnp.tanh(memory))
            state = jnp.concatenate(states, axis=0)
            last_ref[:, span(r)] = state
            c_buf[t + 1, :, span(r)] = jnp.concatenate(memories, axis=0)
            z_buf[t + 1, feat:feat + hid, span(r)] = state.astype(bf16)

    x_copy(0).wait()
    permute(0)

    def trip(i, carry):
        for u in range(FORWARD_UNROLL):
            t = FORWARD_UNROLL * i + u

            @pl.when(t + 1 < steps)
            def _(t=t):
                x_copy(t + 1).wait()

            @pl.when(t + 3 < steps)
            def _(t=t):
                x_copy(t + 3).start()

        for u in range(FORWARD_UNROLL):
            t = FORWARD_UNROLL * i + u
            z_copy(t).start()
            c_copy(t).start()
            step(t)
        return carry

    lax.fori_loop(0, steps // FORWARD_UNROLL, trip, 0)
    outs[6].start()
    for r in range(rows):
        state = last_ref[:, span(r)]
        for j in range(2):
            act = jnp.sum(state * hwt_ref[:, j:j + 1], axis=0, keepdims=True)
            own_ref[j, r:r + 1, :] = act + off_ref[j]
    for j in range(FIELDS):
        to_dn_ref[j * HALO:(j + 1) * HALO, :] = own_ref[j, rows - HALO:, :]
        to_up_ref[j * HALO:(j + 1) * HALO, :] = own_ref[j, :HALO, :]
    for copy in outs[3:6]:
        copy.start()
    for t in range(steps):
        z_copy(t).wait()
        c_copy(t).wait()
    for copy in outs:
        copy.wait()


def shift_rows(value, step):
    return pltpu.roll(value, step % value.shape[0], 0)


def shift_cols(value, step, col_id):
    cols = value.shape[1]
    moved = pltpu.roll(value, step % cols, 1)
    edge = 0 if step > 0 else cols - 1
    return jnp.where(col_id == edge, 0.0, moved)


def water(land_total, own_ref, up_ref, dn_ref, depth_ref):
    rows, cols = depth_ref.shape
    spare = jnp.zeros((rows - HALO, cols), jnp.float32)

    def window(j):
        halo = slice(j * HALO, (j + 1) * HALO)
        return jnp.concatenate([spare, up_ref[halo], own_ref[j], dn_ref[halo], spare], axis=0)

    act0, act1, start, rain, observed, root_slope, code = [window(j) for j in range(FIELDS)]
    is_land = code > 0.5
    land = jnp.where(is_land, 1.0, 0.0)
    sig0 = 0.5 * jnp.tanh(0.5 * act0) + 0.5
    sig1 = 0.5 * jnp.tanh(0.5 * act1) + 0.5
    soft1 = jnp.maximum(act1, 0.0) + jnp.log(1.0 + jnp.exp(-jnp.abs(act1)))
    manning = jnp.where(is_land, 0.03 + 0.27 * sig0, 0.1)
    infil = jnp.where(is_land, soft1, 1.0)
    dt = 1.0 / SUB
    col_id = lax.broadcasted_iota(jnp.int32, code.shape, 1)
    masks = [jnp.where(code == float(d + 1), 1.0, 0.0) for d in range(8)]
    soak = land * jnp.exp(-dt * infil)
    rain_dt = dt * rain
    rate = dt * root_slope / manning

    def arrive(out):
        total = None
        for col_step in (-1, 0, 1):
            part = None
            for d, (rs, cs) in enumerate(compass):
                if cs != col_step:
                    continue
                flow = out * masks[d]
                flow = shift_rows(flow, rs) if rs else flow
                part = flow if part is None else part + flow
            part = shift_cols(part, col_step, col_id) if col_step else part
            total = part if total is None else total + part
        return total

    def collect(grad):
        total = None
        for col_step in (-1, 0, 1):
            base = shift_cols(grad, -col_step, col_id) if col_step else grad
            for d, (rs, cs) in enumerate(compass):
                if cs != col_step:
                    continue
                back = shift_rows(base, -rs) if rs else base
                back = back * masks[d]
                total = back if total is None else total + back
        return total

    level = start
    kept = []
    for _ in range(SUB):
        wet = (level + rain_dt) * soak
        lifted = wet + 0.001
        power = jnp.exp((2.0 / 3.0) * jnp.log(lifted))
        drain = rate * power
        left = jnp.exp(-drain)
        out = wet * (1.0 - left)
        level = land * (wet - out + arrive(out))
        kept.append((wet, lifted, drain, left))
    own = slice(rows, 2 * rows)
    depth_ref[...] = level[own]
    gap = land * (level - observed)
    own_gap = gap[own]
    misfit = jnp.sum(jnp.sum(own_gap * own_gap, axis=1, keepdims=True), axis=0, keepdims=True) * (1.0 / land_total)
    grad = (2.0 / land_total) * land * gap
    g_drain_sum = jnp.zeros_like(grad)
    g_soak_sum = jnp.zeros_like(grad)
    for wet, lifted, drain, left in reversed(kept):
        settled = land * grad
        g_out = collect(settled) - settled
        g_drain = g_out * wet * left * drain
        g_wet = settled + g_out * (1.0 - left) + (2.0 / 3.0) * g_drain / lifted
        g_drain_sum = g_drain_sum + g_drain
        g_soak_sum = g_soak_sum + g_wet * wet
        grad = g_wet * soak
    g_act0 = jnp.where(is_land, -g_drain_sum / manning * (0.27 * sig0 * (1.0 - sig0)), 0.0)[own]
    g_act1 = jnp.where(is_land, -dt * g_soak_sum * sig1, 0.0)[own]
    return g_act0, g_act1, misfit


def head_line(last_ref, gact_ref, misfit):
    rows, cols = gact_ref.shape[1], gact_ref.shape[2]
    hid = last_ref.shape[0]
    sums, totals = [], []
    for j in range(2):
        g = gact_ref[j]
        acc = jnp.zeros((hid, cols), jnp.float32)
        for r in range(rows):
            acc = acc + last_ref[:, r * cols:(r + 1) * cols] * g[r:r + 1, :]
        sums.append(acc)
        totals.append(jnp.sum(jnp.sum(g, axis=1, keepdims=True), axis=0, keepdims=True))
    heads = 0.5 * jnp.sum(jnp.concatenate(sums, axis=0).T, axis=0, keepdims=True)
    lane = lax.broadcasted_iota(jnp.int32, heads.shape, 1)
    rest = jnp.where(lane == 0, totals[0], jnp.where(lane == 1, totals[1], jnp.where(lane == 2, misfit, 0.0)))
    return jnp.concatenate([heads, rest], axis=1)


def backward_kernel(
    land_total, unroll, side_ref, z_hbm, c_hbm, weight_hbm, wback_hbm, hwt_hbm, own_hbm, last_hbm, up_ref, dn_ref,
    depth_ref, keep_ref, send_ref, z_buf, c_buf, weight_ref, wback_ref, hwt_ref, own_ref, last_ref, gact_ref,
    gam_scr, gc_scr, acc_scr, z_sem, c_sem, small_sem,
):
    steps, hid = c_buf.shape[0], c_buf.shape[1]
    rows, cols = depth_ref.shape

    def span(r):
        return slice(r * cols, (r + 1) * cols)

    def z_copy(t):
        return pltpu.make_async_copy(z_hbm.at[t], z_buf.at[t], z_sem.at[t])

    def c_copy(t):
        return pltpu.make_async_copy(c_hbm.at[t], c_buf.at[t], c_sem.at[t])

    pairs = (
        (own_hbm, own_ref), (hwt_hbm, hwt_ref), (weight_hbm, weight_ref), (wback_hbm, wback_ref), (last_hbm, last_ref),
    )
    small = [pltpu.make_async_copy(src, dst, small_sem.at[i]) for i, (src, dst) in enumerate(pairs)]
    for copy in small[:4]:
        copy.start()
    for t in range(steps - 1, steps - 1 - AHEAD * unroll, -1):
        z_copy(t).start()
        c_copy(t).start()
        if t == steps - unroll:
            small[4].start()
    acc_scr[...] = jnp.zeros_like(acc_scr)
    gc_scr[...] = jnp.zeros_like(gc_scr)
    small[0].wait()
    g_act0, g_act1, misfit = water(land_total, own_ref, up_ref, dn_ref, depth_ref)
    gact_ref[0] = g_act0
    gact_ref[1] = g_act1
    for copy in small[1:4]:
        copy.wait()
    for r in range(rows):
        gam_scr[:, span(r)] = 0.5 * (
            hwt_ref[:, 0:1] * gact_ref[0, r:r + 1, :] + hwt_ref[:, 1:2] * gact_ref[1, r:r + 1, :]
        )
    weight = weight_ref[...]
    wback = wback_ref[...]
    order = [(u, r) for u in range(unroll) for r in range(rows)]

    def gates(t, r):
        return jnp.dot(weight, z_buf[t, :, span(r)], preferred_element_type=jnp.float32)

    def spread(t, r, low):
        gam_scr[:, span(r)] = jnp.dot(wback, low, preferred_element_type=jnp.float32)
        acc_scr[...] += lax.dot_general(
            z_buf[t, :, span(r)], low, (((1,), (1,)), ((), ())), preferred_element_type=jnp.float32
        )

    def hours(k, carry):
        top = steps - 1 - unroll * k
        for u in range(unroll):
            later = top - u - AHEAD * unroll

            @pl.when(later >= 0)
            def _(later=later):
                z_copy(later).start()
                c_copy(later).start()

        for u in range(unroll):
            z_copy(top - u).wait()
            c_copy(top - u).wait()
        ahead = gates(top, 0)
        low = None
        for i, (u, r) in enumerate(order):
            a = ahead
            ahead = gates(top - order[i + 1][0], order[i + 1][1]) if i + 1 < len(order) else None
            if low is not None:
                spread(top - order[i - 1][0], order[i - 1][1], low)
            before = c_buf[top - u, :, span(r)]
            gam = gam_scr[:, span(r)]
            carried = gc_scr[:, span(r)]
            lows, passed = [], []
            for g in range(0, hid, GROUP):
                part = slice(g, g + GROUP)
                t_in, t_keep, cand, t_out = cell_gates(a, g)
                p_in = t_in + 1.0
                p_keep = t_keep + 1.0
                held = p_keep * before[part]
                fresh = p_in * cand
                squash = jnp.tanh(0.5 * (held + fresh))
                flow = gam[part] * (t_out + 1.0)
                grad_c = carried[part] + flow * (1.0 - squash * squash)
                e_in = (grad_c * fresh) * (1.0 - t_in)
                e_keep = (grad_c * held) * (1.0 - t_keep)
                e_cand = (grad_c * p_in) * (1.0 - cand * cand)
                e_out = (flow * squash) * (1.0 - t_out)
                passed.append(0.5 * (grad_c * p_keep))
                lows.append(jnp.concatenate([e_in, e_keep, e_cand, e_out], axis=0).astype(jnp.bfloat16))
            gc_scr[:, span(r)] = jnp.concatenate(passed, axis=0)
            low = jnp.concatenate(lows, axis=0)
        spread(top - order[-1][0], order[-1][1], low)
        return carry

    lax.fori_loop(0, steps // unroll, hours, 0)
    small[4].wait()
    line = head_line(last_ref, gact_ref, misfit)
    used = keep_ref.shape[0] - 8
    row = lax.broadcasted_iota(jnp.int32, (8, 4 * hid), 0)
    extra = jnp.where(row == 0, acc_scr[used:used + 1], jnp.where(row == 1, line, 0.0))
    whole = jnp.concatenate([acc_scr[:used], extra], axis=0)
    half = whole.shape[1] // 2
    left, right = whole[:, :half], whole[:, half:]
    first = side_ref[0] == 0
    keep_ref[...] = jnp.where(first, left, right)
    send_ref[...] = jnp.where(first, right, left)


def finish_kernel(feat, side_ref, mine_ref, other_ref, input_ref, hidden_ref, bias_ref, head_ref, offset_ref, misfit_ref):
    hid = hidden_ref.shape[0]
    mine, other = mine_ref[...], other_ref[...]
    first = side_ref[0] == 0
    left = jnp.where(first, mine, other)
    right = jnp.where(first, other, mine)
    whole = jnp.concatenate([left, right], axis=1)
    row = feat + hid + 1
    extra = whole[row:row + 1]
    whole = jnp.concatenate([whole, jnp.zeros((128 - whole.shape[0], 4 * hid), jnp.float32)], axis=0)
    turned = whole.T
    turned = turned * row_scale(turned.shape, hid, (0.5, 0.5, 1.0, 1.0))
    turned = jnp.concatenate(
        [turned[4 * g + q * GROUP:4 * g + (q + 1) * GROUP] for q in range(4) for g in range(0, hid, GROUP)], axis=0
    )
    turned = turned.T
    input_ref[...] = turned[:feat]
    hidden_ref[...] = 0.5 * turned[feat:feat + hid]
    bias_ref[...] = turned[feat + hid:feat + hid + 1]
    head_ref[0:1, :] = extra[:, :hid]
    head_ref[1:2, :] = extra[:, hid:2 * hid]
    offset_ref[...] = extra[:, 2 * hid:2 * hid + 2]
    misfit_ref[...] = extra[:, 2 * hid + 2:2 * hid + 3]


def swap(value, stride):
    count = lax.axis_size("row")
    return lax.ppermute(value, "row", [(i, i ^ stride) for i in range(count)])


def shards(
    forcing, rainfall, depth_start, observed, land_mask, tile_land, land_rank, flow_code, terrain_slope,
    input_weight, hidden_weight, gate_bias, head_weight, head_offset,
):
    steps, feat, rows, cols = forcing.shape
    hid = hidden_weight.shape[1]
    cells = rows * cols
    depth = feat + hid + PAD
    payload = feat + hid + 8
    count = lax.axis_size("row")
    land_total = LAND_DEV * count
    f32, bf16 = jnp.float32, jnp.bfloat16
    vmem = pl.BlockSpec(memory_space=pltpu.VMEM)
    smem = pl.BlockSpec(memory_space=pltpu.SMEM)
    hbm = pl.BlockSpec(memory_space=pl.ANY)
    shape = jax.ShapeDtypeStruct

    ins = (
        input_weight.T, hidden_weight.T, gate_bias.reshape(1, 4 * hid), head_weight,
        land_mask, flow_code, terrain_slope, depth_start, rainfall, observed,
    )
    outs = [
        shape((4 * hid, depth), bf16),
        shape((hid, 4 * hid), bf16),
        shape((hid, 128), f32),
        shape((FIELDS, rows, cols), f32),
        shape((FIELDS * HALO, cols), f32),
        shape((FIELDS * HALO, cols), f32),
        shape((hid, cells), f32),
    ]
    z_all, c_all, weight, wback, hwt, own, to_dn, to_up, last = pl.pallas_call(
        forward_kernel,
        in_specs=[hbm, smem] + [hbm] * INS,
        out_specs=[hbm] * (2 + OUTS),
        out_shape=[shape((steps, depth, cells), bf16), shape((steps, hid, cells), f32)] + outs,
        scratch_shapes=[pltpu.VMEM(item.shape, item.dtype) for item in (*ins, *outs)]
        + [
            pltpu.VMEM((steps, feat * rows, cols), bf16),
            pltpu.VMEM((steps + 1, depth, cells), bf16),
            pltpu.VMEM((steps + 1, hid, cells), f32),
            pltpu.VMEM((feat * rows, feat * rows), bf16),
            pltpu.SemaphoreType.DMA((steps,)),
            pltpu.SemaphoreType.DMA((steps,)),
            pltpu.SemaphoreType.DMA((steps,)),
            pltpu.SemaphoreType.DMA((INS,)),
            pltpu.SemaphoreType.DMA((OUTS,)),
        ],
        compiler_params=pltpu.CompilerParams(vmem_limit_bytes=56 << 20),
    )(forcing.reshape(steps, feat * rows, cols), head_offset, *ins)

    from_up = lax.ppermute(to_dn, "row", [(i, i + 1) for i in range(count - 1)])
    from_dn = lax.ppermute(to_up, "row", [(i + 1, i) for i in range(count - 1)])

    side = (lax.axis_index("row") % 2).astype(jnp.int32).reshape(1)
    def backward(*refs):
        backward_kernel(land_total, 2, *refs)

    depth_final, keep, send = pl.pallas_call(
        backward,
        in_specs=[smem] + [hbm] * 7 + [vmem] * 2,
        out_specs=[vmem] * 3,
        out_shape=[shape((rows, cols), f32), shape((payload, 2 * hid), f32), shape((payload, 2 * hid), f32)],
        scratch_shapes=[
            pltpu.VMEM((steps, depth, cells), bf16),
            pltpu.VMEM((steps, hid, cells), f32),
            pltpu.VMEM((4 * hid, depth), bf16),
            pltpu.VMEM((hid, 4 * hid), bf16),
            pltpu.VMEM((hid, 128), f32),
            pltpu.VMEM((FIELDS, rows, cols), f32),
            pltpu.VMEM((hid, cells), f32),
            pltpu.VMEM((2, rows, cols), f32),
            pltpu.VMEM((hid, cells), f32),
            pltpu.VMEM((hid, cells), f32),
            pltpu.VMEM((depth, 4 * hid), f32),
            pltpu.SemaphoreType.DMA((steps,)),
            pltpu.SemaphoreType.DMA((steps,)),
            pltpu.SemaphoreType.DMA((5,)),
        ],
        compiler_params=pltpu.CompilerParams(vmem_limit_bytes=56 << 20),
    )(side, z_all, c_all, weight, wback, hwt, own, last, from_up, from_dn)

    mine = keep + swap(send, 1)
    stride = 2
    while stride < count:
        mine = mine + swap(mine, stride)
        stride *= 2
    other = swap(mine, 1)

    def finish(*refs):
        finish_kernel(feat, *refs)

    grads = pl.pallas_call(
        finish,
        in_specs=[smem, vmem, vmem],
        out_specs=[vmem] * 6,
        out_shape=[
            shape((feat, 4 * hid), f32),
            shape((hid, 4 * hid), f32),
            shape((1, 4 * hid), f32),
            shape((2, hid), f32),
            shape((1, 2), f32),
            shape((1, 1), f32),
        ],
        compiler_params=pltpu.CompilerParams(vmem_limit_bytes=32 << 20),
    )(side, mine, other)
    return (
        depth_final, grads[5].reshape(1), grads[0].T, grads[1].T, grads[2].reshape(4 * hid), grads[3], grads[4].reshape(2),
    )


def solution(mesh):
    return jax.shard_map(
        shards,
        mesh=mesh,
        in_specs=(
            P(None, None, ("groups", "row"), None),
            P(("groups", "row"), None),
            P(("groups", "row"), None),
            P(("groups", "row"), None),
            P("row", None),
            P(),
            P("row", None),
            P("row", None),
            P("row", None),
            P(),
            P(),
            P(),
            P(),
            P(),
        ),
        out_specs=(
            P(("groups", "row"), None),
            P("groups"),
            P("groups", None),
            P("groups", None),
            P("groups"),
            P("groups", None),
            P("groups"),
        ),
        check_vma=False,
    )
```

```python
import jax
import jax.numpy as jnp
from jax import lax
from jax.experimental import pallas as pl
from jax.experimental.pallas import tpu as pltpu
from jax.sharding import PartitionSpec as P

SUB = 6
LAND_DEV = 2048
PAD = 16
HALO = 2 * SUB
FIELDS = 7
GROUP = 8
AHEAD = 1
FORWARD_UNROLL = 2
INS = 10
OUTS = 7

compass = ((-1, -1), (-1, 0), (-1, 1), (0, -1), (0, 1), (1, -1), (1, 0), (1, 1))


def gate_rows(array, hid):
    return jnp.concatenate(
        [array[q * hid + g:q * hid + g + GROUP] for g in range(0, hid, GROUP) for q in range(4)], axis=0
    )


def row_scale(shape, hid, values):
    row = lax.broadcasted_iota(jnp.int32, shape, 0) % (4 * GROUP) // GROUP
    return jnp.where(row == 0, values[0], jnp.where(row == 1, values[1], jnp.where(row == 2, values[2], values[3])))


def cell_gates(a, g):
    base = 4 * g
    return [jnp.tanh(a[base + q * GROUP:base + (q + 1) * GROUP]) for q in range(4)]


def forward_kernel(x_hbm, off_ref, *refs):
    in_hbm, (z_hbm, c_hbm), out_hbm = refs[:INS], refs[INS:INS + 2], refs[INS + 2:INS + 2 + OUTS]
    in_buf, out_buf = refs[INS + 2 + OUTS:2 * INS + 2 + OUTS], refs[2 * INS + 2 + OUTS:2 * INS + 2 + 2 * OUTS]
    x_buf, z_buf, c_buf, perm_scr, x_sem, z_sem, c_sem, in_sem, out_sem = refs[2 * INS + 2 + 2 * OUTS:]
    input_ref, hidden_ref, bias_ref, head_ref, mask_ref, flow_ref, slope_ref, start_ref, rain_ref, observed_ref = in_buf
    weight_ref, wback_ref, hwt_ref, own_ref, to_dn_ref, to_up_ref, last_ref = out_buf
    steps = x_buf.shape[0]
    rows, cols = start_ref.shape
    feat = input_ref.shape[0]
    hid = hidden_ref.shape[0]
    cells = rows * cols
    depth = feat + hid + PAD
    f32, bf16 = jnp.float32, jnp.bfloat16
    ins = [pltpu.make_async_copy(in_hbm[i], in_buf[i], in_sem.at[i]) for i in range(INS)]
    outs = [pltpu.make_async_copy(out_buf[i], out_hbm[i], out_sem.at[i]) for i in range(OUTS)]
    for copy in ins:
        copy.start()

    def x_copy(t):
        return pltpu.make_async_copy(x_hbm.at[t], x_buf.at[t], x_sem.at[t])

    def z_copy(t):
        return pltpu.make_async_copy(z_buf.at[t], z_hbm.at[t], z_sem.at[t])

    def c_copy(t):
        return pltpu.make_async_copy(c_buf.at[t], c_hbm.at[t], c_sem.at[t])

    def span(r):
        return slice(r * cols, (r + 1) * cols)

    for t in range(3):
        x_copy(t).start()

    shape = perm_scr.shape
    place = lax.broadcasted_iota(jnp.int32, (shape[0], 1), 0)
    source = place % feat * rows + place // feat
    perm_scr[...] = jnp.where(source == lax.broadcasted_iota(jnp.int32, shape, 1), 1.0, 0.0).astype(bf16)
    for copy in ins:
        copy.wait()
    own_ref[2] = start_ref[...]
    own_ref[3] = rain_ref[...]
    own_ref[4] = observed_ref[...]
    own_ref[5] = jnp.sqrt(slope_ref[...])
    own_ref[6] = jnp.where(mask_ref[...] == 1, flow_ref[...] + 1, 0).astype(f32)
    bias = jnp.broadcast_to(bias_ref[...], (128 - feat - hid, 4 * hid))
    bias = jnp.where(lax.broadcasted_iota(jnp.int32, bias.shape, 0) < 3, bias, 0.0)
    weight = gate_rows(jnp.concatenate([input_ref[...].astype(f32), hidden_ref[...].astype(f32), bias], axis=0).T, hid)
    col_id = lax.broadcasted_iota(jnp.int32, weight.shape, 1)
    back = jnp.where(col_id < feat + hid, weight, 0.0) * row_scale(weight.shape, hid, (0.125, 0.125, 0.25, 0.25))
    wback_ref[...] = back.T[feat:feat + hid].astype(bf16)
    weight = weight * row_scale(weight.shape, hid, (0.5, 0.5, 1.0, 0.5))
    weight = jnp.where((col_id >= feat) & (col_id < feat + hid), 0.5 * weight, weight)
    high = weight.astype(bf16).astype(f32)
    middle = (weight - high).astype(bf16).astype(f32)
    low = weight - high - middle
    weight = jnp.where(col_id == feat + hid + 1, middle, jnp.where(col_id == feat + hid + 2, low, weight))
    weight_ref[...] = weight[:, :depth].astype(bf16)
    head = jnp.concatenate([head_ref[...], jnp.zeros((126, hid), f32)], axis=0)
    head = jnp.concatenate([head, jnp.zeros((128, 128 - hid), f32)], axis=1)
    hwt_ref[...] = 0.5 * head.T[:hid]

    for copy in outs[:3]:
        copy.start()
    c_buf[0] = jnp.zeros((hid, cells), f32)
    z_buf[0, feat:feat + hid, :] = jnp.zeros((hid, cells), bf16)
    ones = jnp.where(lax.broadcasted_iota(jnp.int32, (PAD, cells), 0) < 3, 1.0, 0.0).astype(bf16)

    def permute(t):
        moved = jnp.dot(perm_scr[...], x_buf[jnp.minimum(t, steps - 1)], preferred_element_type=f32).astype(bf16)
        for r in range(rows):
            z_buf[t, :feat, span(r)] = moved[r * feat:(r + 1) * feat]
        z_buf[t, feat + hid:, :] = ones

    def step(t):
        weight = weight_ref[...]

        def gates(r):
            return jnp.dot(weight, z_buf[t, :, span(r)], preferred_element_type=f32)

        ahead = gates(0)
        for r in range(rows):
            a = ahead
            ahead = gates(r + 1) if r + 1 < rows else None
            if r == rows // 2:
                permute(t + 1)
            before = c_buf[t, :, span(r)]
            memories, states = [], []
            for g in range(0, hid, GROUP):
                t_in, t_keep, cand, t_out = cell_gates(a, g)
                memory = 0.5 * ((t_keep + 1.0) * before[g:g + GROUP] + (t_in + 1.0) * cand)
                memories.append(memory)
                states.append((t_out + 1.0) * jnp.tanh(memory))
            state = jnp.concatenate(states, axis=0)
            last_ref[:, span(r)] = state
            c_buf[t + 1, :, span(r)] = jnp.concatenate(memories, axis=0)
            z_buf[t + 1, feat:feat + hid, span(r)] = state.astype(bf16)

    x_copy(0).wait()
    permute(0)

    def trip(i, carry):
        for u in range(FORWARD_UNROLL):
            t = FORWARD_UNROLL * i + u

            @pl.when(t + 1 < steps)
            def _(t=t):
                x_copy(t + 1).wait()

            @pl.when(t + 3 < steps)
            def _(t=t):
                x_copy(t + 3).start()

        for u in range(FORWARD_UNROLL):
            t = FORWARD_UNROLL * i + u
            z_copy(t).start()
            c_copy(t).start()
            step(t)
        return carry

    lax.fori_loop(0, steps // FORWARD_UNROLL, trip, 0)
    outs[6].start()
    for r in range(rows):
        state = last_ref[:, span(r)]
        for j in range(2):
            act = jnp.sum(state * hwt_ref[:, j:j + 1], axis=0, keepdims=True)
            own_ref[j, r:r + 1, :] = act + off_ref[j]
    for j in range(FIELDS):
        to_dn_ref[j * HALO:(j + 1) * HALO, :] = own_ref[j, rows - HALO:, :]
        to_up_ref[j * HALO:(j + 1) * HALO, :] = own_ref[j, :HALO, :]
    for copy in outs[3:6]:
        copy.start()
    for t in range(steps):
        z_copy(t).wait()
        c_copy(t).wait()
    for copy in outs:
        copy.wait()


def shift_rows(value, step):
    return pltpu.roll(value, step % value.shape[0], 0)


def shift_cols(value, step, col_id):
    cols = value.shape[1]
    moved = pltpu.roll(value, step % cols, 1)
    edge = 0 if step > 0 else cols - 1
    return jnp.where(col_id == edge, 0.0, moved)


def water(land_total, own_ref, up_ref, dn_ref, depth_ref):
    rows, cols = depth_ref.shape
    spare = jnp.zeros((rows - HALO, cols), jnp.float32)

    def window(j):
        halo = slice(j * HALO, (j + 1) * HALO)
        return jnp.concatenate([spare, up_ref[halo], own_ref[j], dn_ref[halo], spare], axis=0)

    act0, act1, start, rain, observed, root_slope, code = [window(j) for j in range(FIELDS)]
    is_land = code > 0.5
    land = jnp.where(is_land, 1.0, 0.0)
    sig0 = 0.5 * jnp.tanh(0.5 * act0) + 0.5
    sig1 = 0.5 * jnp.tanh(0.5 * act1) + 0.5
    soft1 = jnp.maximum(act1, 0.0) + jnp.log(1.0 + jnp.exp(-jnp.abs(act1)))
    manning = jnp.where(is_land, 0.03 + 0.27 * sig0, 0.1)
    infil = jnp.where(is_land, soft1, 1.0)
    dt = 1.0 / SUB
    col_id = lax.broadcasted_iota(jnp.int32, code.shape, 1)
    masks = [jnp.where(code == float(d + 1), 1.0, 0.0) for d in range(8)]
    soak = land * jnp.exp(-dt * infil)
    rain_dt = dt * rain
    rate = dt * root_slope / manning

    def arrive(out):
        total = None
        for col_step in (-1, 0, 1):
            part = None
            for d, (rs, cs) in enumerate(compass):
                if cs != col_step:
                    continue
                flow = out * masks[d]
                flow = shift_rows(flow, rs) if rs else flow
                part = flow if part is None else part + flow
            part = shift_cols(part, col_step, col_id) if col_step else part
            total = part if total is None else total + part
        return total

    def collect(grad):
        total = None
        for col_step in (-1, 0, 1):
            base = shift_cols(grad, -col_step, col_id) if col_step else grad
            for d, (rs, cs) in enumerate(compass):
                if cs != col_step:
                    continue
                back = shift_rows(base, -rs) if rs else base
                back = back * masks[d]
                total = back if total is None else total + back
        return total

    level = start
    kept = []
    for _ in range(SUB):
        wet = (level + rain_dt) * soak
        lifted = wet + 0.001
        power = jnp.exp((2.0 / 3.0) * jnp.log(lifted))
        drain = rate * power
        left = jnp.exp(-drain)
        out = wet * (1.0 - left)
        level = land * (wet - out + arrive(out))
        kept.append((wet, lifted, drain, left))
    own = slice(rows, 2 * rows)
    depth_ref[...] = level[own]
    gap = land * (level - observed)
    own_gap = gap[own]
    misfit = jnp.sum(jnp.sum(own_gap * own_gap, axis=1, keepdims=True), axis=0, keepdims=True) * (1.0 / land_total)
    grad = (2.0 / land_total) * land * gap
    g_drain_sum = jnp.zeros_like(grad)
    g_soak_sum = jnp.zeros_like(grad)
    for wet, lifted, drain, left in reversed(kept):
        settled = land * grad
        g_out = collect(settled) - settled
        g_drain = g_out * wet * left * drain
        g_wet = settled + g_out * (1.0 - left) + (2.0 / 3.0) * g_drain / lifted
        g_drain_sum = g_drain_sum + g_drain
        g_soak_sum = g_soak_sum + g_wet * wet
        grad = g_wet * soak
    g_act0 = jnp.where(is_land, -g_drain_sum / manning * (0.27 * sig0 * (1.0 - sig0)), 0.0)[own]
    g_act1 = jnp.where(is_land, -dt * g_soak_sum * sig1, 0.0)[own]
    return g_act0, g_act1, misfit


def head_line(last_ref, gact_ref, misfit):
    rows, cols = gact_ref.shape[1], gact_ref.shape[2]
    hid = last_ref.shape[0]
    sums, totals = [], []
    for j in range(2):
        g = gact_ref[j]
        acc = jnp.zeros((hid, cols), jnp.float32)
        for r in range(rows):
            acc = acc + last_ref[:, r * cols:(r + 1) * cols] * g[r:r + 1, :]
        sums.append(acc)
        totals.append(jnp.sum(jnp.sum(g, axis=1, keepdims=True), axis=0, keepdims=True))
    heads = 0.5 * jnp.sum(jnp.concatenate(sums, axis=0).T, axis=0, keepdims=True)
    lane = lax.broadcasted_iota(jnp.int32, heads.shape, 1)
    rest = jnp.where(lane == 0, totals[0], jnp.where(lane == 1, totals[1], jnp.where(lane == 2, misfit, 0.0)))
    return jnp.concatenate([heads, rest], axis=1)


def backward_kernel(
    land_total, unroll, side_ref, z_hbm, c_hbm, weight_hbm, wback_hbm, hwt_hbm, own_hbm, last_hbm, up_hbm, dn_hbm,
    depth_ref, keep_ref, send_ref, z_buf, c_buf, weight_ref, wback_ref, hwt_ref, own_ref, last_ref, up_ref, dn_ref,
    gact_ref, gam_scr, gc_scr, acc_scr, z_sem, c_sem, small_sem,
):
    steps, hid = c_buf.shape[0], c_buf.shape[1]
    rows, cols = depth_ref.shape

    def span(r):
        return slice(r * cols, (r + 1) * cols)

    def z_copy(t):
        return pltpu.make_async_copy(z_hbm.at[t], z_buf.at[t], z_sem.at[t])

    def c_copy(t):
        return pltpu.make_async_copy(c_hbm.at[t], c_buf.at[t], c_sem.at[t])

    pairs = (
        (own_hbm, own_ref), (up_hbm, up_ref), (dn_hbm, dn_ref), (hwt_hbm, hwt_ref), (weight_hbm, weight_ref),
        (wback_hbm, wback_ref), (last_hbm, last_ref),
    )
    small = [pltpu.make_async_copy(src, dst, small_sem.at[i]) for i, (src, dst) in enumerate(pairs)]
    for copy in small[:6]:
        copy.start()
    for t in range(steps - 1, steps - 1 - AHEAD * unroll, -1):
        z_copy(t).start()
        c_copy(t).start()
        if t == steps - unroll:
            small[6].start()
    acc_scr[...] = jnp.zeros_like(acc_scr)
    gc_scr[...] = jnp.zeros_like(gc_scr)
    for copy in small[:3]:
        copy.wait()
    g_act0, g_act1, misfit = water(land_total, own_ref, up_ref, dn_ref, depth_ref)
    gact_ref[0] = g_act0
    gact_ref[1] = g_act1
    for copy in small[3:6]:
        copy.wait()
    for r in range(rows):
        gam_scr[:, span(r)] = 0.5 * (
            hwt_ref[:, 0:1] * gact_ref[0, r:r + 1, :] + hwt_ref[:, 1:2] * gact_ref[1, r:r + 1, :]
        )
    weight = weight_ref[...]
    wback = wback_ref[...]
    order = [(u, r) for u in range(unroll) for r in range(rows)]

    def gates(t, r):
        return jnp.dot(weight, z_buf[t, :, span(r)], preferred_element_type=jnp.float32)

    def spread(t, r, low):
        gam_scr[:, span(r)] = jnp.dot(wback, low, preferred_element_type=jnp.float32)
        acc_scr[...] += lax.dot_general(
            z_buf[t, :, span(r)], low, (((1,), (1,)), ((), ())), preferred_element_type=jnp.float32
        )

    def hours(k, carry):
        top = steps - 1 - unroll * k
        for u in range(unroll):
            later = top - u - AHEAD * unroll

            @pl.when(later >= 0)
            def _(later=later):
                z_copy(later).start()
                c_copy(later).start()

        for u in range(unroll):
            z_copy(top - u).wait()
            c_copy(top - u).wait()
        ahead = gates(top, 0)
        low = None
        for i, (u, r) in enumerate(order):
            a = ahead
            ahead = gates(top - order[i + 1][0], order[i + 1][1]) if i + 1 < len(order) else None
            before = c_buf[top - u, :, span(r)]
            gam = gam_scr[:, span(r)]
            carried = gc_scr[:, span(r)]
            lows, passed = [], []
            for g in range(0, hid, GROUP):
                part = slice(g, g + GROUP)
                t_in, t_keep, cand, t_out = cell_gates(a, g)
                p_in = t_in + 1.0
                p_keep = t_keep + 1.0
                held = p_keep * before[part]
                fresh = p_in * cand
                squash = jnp.tanh(0.5 * (held + fresh))
                flow = gam[part] * (t_out + 1.0)
                grad_c = carried[part] + flow * (1.0 - squash * squash)
                e_in = (grad_c * fresh) * (1.0 - t_in)
                e_keep = (grad_c * held) * (1.0 - t_keep)
                e_cand = (grad_c * p_in) * (1.0 - cand * cand)
                e_out = (flow * squash) * (1.0 - t_out)
                passed.append(0.5 * (grad_c * p_keep))
                lows.append(jnp.concatenate([e_in, e_keep, e_cand, e_out], axis=0).astype(jnp.bfloat16))
            gc_scr[:, span(r)] = jnp.concatenate(passed, axis=0)
            if low is not None:
                spread(top - order[i - 1][0], order[i - 1][1], low)
            low = jnp.concatenate(lows, axis=0)
        spread(top - order[-1][0], order[-1][1], low)
        return carry

    lax.fori_loop(0, steps // unroll, hours, 0)
    small[6].wait()
    line = head_line(last_ref, gact_ref, misfit)
    used = keep_ref.shape[0] - 8
    row = lax.broadcasted_iota(jnp.int32, (8, 4 * hid), 0)
    extra = jnp.where(row == 0, acc_scr[used:used + 1], jnp.where(row == 1, line, 0.0))
    whole = jnp.concatenate([acc_scr[:used], extra], axis=0)
    half = whole.shape[1] // 2
    left, right = whole[:, :half], whole[:, half:]
    first = side_ref[0] == 0
    keep_ref[...] = jnp.where(first, left, right)
    send_ref[...] = jnp.where(first, right, left)


def finish_kernel(feat, side_ref, mine_ref, other_ref, input_ref, hidden_ref, bias_ref, head_ref, offset_ref, misfit_ref):
    hid = hidden_ref.shape[0]
    mine, other = mine_ref[...], other_ref[...]
    first = side_ref[0] == 0
    left = jnp.where(first, mine, other)
    right = jnp.where(first, other, mine)
    whole = jnp.concatenate([left, right], axis=1)
    row = feat + hid + 1
    extra = whole[row:row + 1]
    whole = jnp.concatenate([whole, jnp.zeros((128 - whole.shape[0], 4 * hid), jnp.float32)], axis=0)
    turned = whole.T
    turned = turned * row_scale(turned.shape, hid, (0.5, 0.5, 1.0, 1.0))
    turned = jnp.concatenate(
        [turned[4 * g + q * GROUP:4 * g + (q + 1) * GROUP] for q in range(4) for g in range(0, hid, GROUP)], axis=0
    )
    turned = turned.T
    input_ref[...] = turned[:feat]
    hidden_ref[...] = 0.5 * turned[feat:feat + hid]
    bias_ref[...] = turned[feat + hid:feat + hid + 1]
    head_ref[0:1, :] = extra[:, :hid]
    head_ref[1:2, :] = extra[:, hid:2 * hid]
    offset_ref[...] = extra[:, 2 * hid:2 * hid + 2]
    misfit_ref[...] = extra[:, 2 * hid + 2:2 * hid + 3]


def swap(value, stride):
    count = lax.axis_size("row")
    return lax.ppermute(value, "row", [(i, i ^ stride) for i in range(count)])


def shards(
    forcing, rainfall, depth_start, observed, land_mask, tile_land, land_rank, flow_code, terrain_slope,
    input_weight, hidden_weight, gate_bias, head_weight, head_offset,
):
    steps, feat, rows, cols = forcing.shape
    hid = hidden_weight.shape[1]
    cells = rows * cols
    depth = feat + hid + PAD
    payload = feat + hid + 8
    count = lax.axis_size("row")
    land_total = LAND_DEV * count
    f32, bf16 = jnp.float32, jnp.bfloat16
    vmem = pl.BlockSpec(memory_space=pltpu.VMEM)
    smem = pl.BlockSpec(memory_space=pltpu.SMEM)
    hbm = pl.BlockSpec(memory_space=pl.ANY)
    shape = jax.ShapeDtypeStruct

    ins = (
        input_weight.T, hidden_weight.T, gate_bias.reshape(1, 4 * hid), head_weight,
        land_mask, flow_code, terrain_slope, depth_start, rainfall, observed,
    )
    outs = [
        shape((4 * hid, depth), bf16),
        shape((hid, 4 * hid), bf16),
        shape((hid, 128), f32),
        shape((FIELDS, rows, cols), f32),
        shape((FIELDS * HALO, cols), f32),
        shape((FIELDS * HALO, cols), f32),
        shape((hid, cells), f32),
    ]
    z_all, c_all, weight, wback, hwt, own, to_dn, to_up, last = pl.pallas_call(
        forward_kernel,
        in_specs=[hbm, smem] + [hbm] * INS,
        out_specs=[hbm] * (2 + OUTS),
        out_shape=[shape((steps, depth, cells), bf16), shape((steps, hid, cells), f32)] + outs,
        scratch_shapes=[pltpu.VMEM(item.shape, item.dtype) for item in (*ins, *outs)]
        + [
            pltpu.VMEM((steps, feat * rows, cols), bf16),
            pltpu.VMEM((steps + 1, depth, cells), bf16),
            pltpu.VMEM((steps + 1, hid, cells), f32),
            pltpu.VMEM((feat * rows, feat * rows), bf16),
            pltpu.SemaphoreType.DMA((steps,)),
            pltpu.SemaphoreType.DMA((steps,)),
            pltpu.SemaphoreType.DMA((steps,)),
            pltpu.SemaphoreType.DMA((INS,)),
            pltpu.SemaphoreType.DMA((OUTS,)),
        ],
        compiler_params=pltpu.CompilerParams(vmem_limit_bytes=56 << 20),
    )(forcing.reshape(steps, feat * rows, cols), head_offset, *ins)

    from_up = lax.ppermute(to_dn, "row", [(i, i + 1) for i in range(count - 1)])
    from_dn = lax.ppermute(to_up, "row", [(i + 1, i) for i in range(count - 1)])

    side = (lax.axis_index("row") % 2).astype(jnp.int32).reshape(1)
    def backward(*refs):
        backward_kernel(land_total, 2, *refs)

    depth_final, keep, send = pl.pallas_call(
        backward,
        in_specs=[smem] + [hbm] * 9,
        out_specs=[vmem] * 3,
        out_shape=[shape((rows, cols), f32), shape((payload, 2 * hid), f32), shape((payload, 2 * hid), f32)],
        scratch_shapes=[
            pltpu.VMEM((steps, depth, cells), bf16),
            pltpu.VMEM((steps, hid, cells), f32),
            pltpu.VMEM((4 * hid, depth), bf16),
            pltpu.VMEM((hid, 4 * hid), bf16),
            pltpu.VMEM((hid, 128), f32),
            pltpu.VMEM((FIELDS, rows, cols), f32),
            pltpu.VMEM((hid, cells), f32),
            pltpu.VMEM((FIELDS * HALO, cols), f32),
            pltpu.VMEM((FIELDS * HALO, cols), f32),
            pltpu.VMEM((2, rows, cols), f32),
            pltpu.VMEM((hid, cells), f32),
            pltpu.VMEM((hid, cells), f32),
            pltpu.VMEM((depth, 4 * hid), f32),
            pltpu.SemaphoreType.DMA((steps,)),
            pltpu.SemaphoreType.DMA((steps,)),
            pltpu.SemaphoreType.DMA((7,)),
        ],
        compiler_params=pltpu.CompilerParams(vmem_limit_bytes=56 << 20),
    )(side, z_all, c_all, weight, wback, hwt, own, last, from_up, from_dn)

    mine = keep + swap(send, 1)
    stride = 2
    while stride < count:
        mine = mine + swap(mine, stride)
        stride *= 2
    other = swap(mine, 1)

    def finish(*refs):
        finish_kernel(feat, *refs)

    grads = pl.pallas_call(
        finish,
        in_specs=[smem, vmem, vmem],
        out_specs=[vmem] * 6,
        out_shape=[
            shape((feat, 4 * hid), f32),
            shape((hid, 4 * hid), f32),
            shape((1, 4 * hid), f32),
            shape((2, hid), f32),
            shape((1, 2), f32),
            shape((1, 1), f32),
        ],
        compiler_params=pltpu.CompilerParams(vmem_limit_bytes=32 << 20),
    )(side, mine, other)
    return (
        depth_final, grads[5].reshape(1), grads[0].T, grads[1].T, grads[2].reshape(4 * hid), grads[3], grads[4].reshape(2),
    )


def solution(mesh):
    return jax.shard_map(
        shards,
        mesh=mesh,
        in_specs=(
            P(None, None, ("groups", "row"), None),
            P(("groups", "row"), None),
            P(("groups", "row"), None),
            P(("groups", "row"), None),
            P("row", None),
            P(),
            P("row", None),
            P("row", None),
            P("row", None),
            P(),
            P(),
            P(),
            P(),
            P(),
        ),
        out_specs=(
            P(("groups", "row"), None),
            P("groups"),
            P("groups", None),
            P("groups", None),
            P("groups"),
            P("groups", None),
            P("groups"),
        ),
        check_vma=False,
    )
```
